32 devices in a mesh: blk: 2 (over x), wide: 16 (over z, y, core).
Axes of the slice: x: 2, y: 2, z: 4, core: 2. Of those that a mesh axis runs over, the one named last changes fastest.
Arguments:
- resid: bfloat16 [8192, 1024], P('wide', 'blk'), may hold values from -24 to 24
- samples: bfloat16 [8192, 1024], P('wide', 'blk'), may hold values from -6 to 6
- precision: float32 [64, 2, 32, 128, 128], P('wide', 'blk'), as said below
- active: int32 [64, 2, 32], P('wide', 'blk'), may hold values 0 or 1
Outputs:
- updated: float32 [64, 2, 32, 128, 128], P('wide', 'blk')
The draws below stay inside these ranges and needn't reach their ends.
Inputs may be any that keep to these rules, and one draw needn't show every extreme that they name: `precision`: entries on the diagonal of W lie between 1 and 2.
All inputs are finite; a program needn't handle non-finite values. No bound on the sum of `active` on one device may be relied on, other than what follows from the above.
Results may differ from the reference program's by a relative error of at most 0.0003.
Values may be sent and summed in bfloat16 or wider, within the bound.
A program may use at most 192 MiB of HBM per device.

```python
import jax
import jax.numpy as jnp
from jax import lax

P_SIZE = 8192
TILE = 128
N = 1024
TILES = 64
TPC = 32
N_BLK = 2


def draw_precision(key, part):
    first_key, second_key = jax.random.split(key, 2)
    full_shape = (TILES, N_BLK, TPC, TILE, TILE)
    off_part = 0.1 * jax.random.normal(first_key, full_shape, jnp.float32)
    diag_part = jax.random.uniform(second_key, full_shape, jnp.float32, 1.0, 2.0)
    row_tile = lax.broadcasted_iota(jnp.int32, full_shape, 0)
    class_index = lax.broadcasted_iota(jnp.int32, full_shape, 1)
    within_index = lax.broadcasted_iota(jnp.int32, full_shape, 2)
    inner_row = lax.broadcasted_iota(jnp.int32, full_shape, 3)
    inner_column = lax.broadcasted_iota(jnp.int32, full_shape, 4)
    column_tile = (class_index - row_tile) % N_BLK + N_BLK * within_index
    on_diag = (column_tile == row_tile) & (inner_row == inner_column)
    return jnp.where(on_diag, diag_part, off_part)


def place_ends(drawn, rng, low, top_value):
    place = [jax.random.randint(jax.random.fold_in(rng, axis), (), 0, length) for axis, length in enumerate(drawn.shape)]
    main_axis = drawn.shape.index(max(drawn.shape))
    neighbour = place[:main_axis] + [(place[main_axis] + 1) % drawn.shape[main_axis]] + place[main_axis + 1:]
    return drawn.at[tuple(place)].set(low).at[tuple(neighbour)].set(top_value)


def block_levels(stream_key, dims, shards, smallest, top_value):
    def one(dim, parts):
        steps = jax.random.uniform(jax.random.fold_in(jax.random.fold_in(stream_key, 6), dim), (parts,), jnp.float32, smallest / len(shards), top_value / len(shards))
        return jnp.repeat(jnp.exp(steps), dims[dim] // parts).reshape((-1,) + (1,) * (len(dims) - dim - 1))

    gain = one(*shards[0])
    for cut in shards[1:]:
        gain = gain * one(*cut)
    return gain


def scatter_about(own_key, dims, deviation, most, shards=(), kind=jnp.bfloat16):
    result = deviation * jax.random.normal(own_key, dims, jnp.float32)
    if shards:
        result = result * block_levels(own_key, dims, shards, -0.22, 0.18)
    return jnp.clip(result, -most, most).astype(kind)


def setup_inputs(seed: int = 0) -> dict:
    seeds = jax.random.split(jax.random.key(seed), 5)
    return {
        "resid": scatter_about(seeds[0], (P_SIZE, N), 4.0, 24.0, ((0, 16), (1, 2))),
        "samples": scatter_about(seeds[1], (P_SIZE, N), 1.0, 6.0, ((0, 16), (1, 2))),
        "precision": draw_precision(jax.random.fold_in(seeds[4], 71), 0),
        "active": place_ends((jax.random.randint(seeds[3], (TILES, N_BLK, TPC), 0, 4) < 3).astype(jnp.int32), jax.random.fold_in(seeds[3], 1), 0, 1),
    }


STEP = 1.0
LASSO = 0.1
RIDGE = 0.5


def class_columns(row_ids, groups, per_class):
    classes = jnp.arange(groups, dtype=jnp.int32)
    within = jnp.arange(per_class, dtype=jnp.int32)
    return (classes[None, :, None] - row_ids[:, None, None]) % groups + groups * within[None, None, :]


def reference(resid, samples, precision, active):
    total_samples = resid.shape[1]
    tiles = precision.shape[0]
    groups = precision.shape[1]
    per_class = precision.shape[2]
    tile_size = precision.shape[3]
    gram = jnp.dot(resid, samples.T, preferred_element_type=jnp.float32) / total_samples
    gram_tiles = gram.reshape(tiles, tile_size, tiles, tile_size).transpose(0, 2, 1, 3)
    row_ids = jnp.arange(tiles, dtype=jnp.int32)
    column_ids = class_columns(row_ids, groups, per_class)
    forward = gram_tiles[row_ids[:, None, None], column_ids]
    backward = jnp.swapaxes(gram_tiles[column_ids, row_ids[:, None, None]], 3, 4)
    symmetric = 0.5 * (forward + backward)
    same_tile = column_ids == row_ids[:, None, None]
    identity = jnp.eye(tile_size, dtype=bool)
    on_diag = same_tile[:, :, :, None, None] & identity
    inverse = jnp.where(on_diag, 1.0 / jnp.where(on_diag, precision, 1.0), 0.0)
    stepped = precision - STEP * (symmetric + RIDGE * precision - inverse)
    shrunk = jnp.sign(stepped) * jnp.maximum(jnp.abs(stepped) - STEP * LASSO, 0.0)
    active_flags = active.astype(precision.dtype)
    return jnp.where(on_diag, stepped, shrunk) * active_flags[:, :, :, None, None]
```

```python
import functools

import jax
import jax.numpy as jnp
from jax import lax
from jax.experimental import pallas as pl
from jax.experimental.pallas import tpu as pltpu
from jax.sharding import PartitionSpec as P

STEP = 1.0
LASSO = 0.1
RIDGE = 0.5


def local(resid, samples, precision, active):
    groups = lax.axis_size("blk")
    column_group = lax.axis_index("blk")
    panel_index = lax.axis_index("wide")
    row_tiles = precision.shape[0]
    per_class = precision.shape[2]
    tile_size = precision.shape[3]
    tiles = per_class * groups
    local_samples = resid.shape[1]
    total_samples = local_samples * groups
    own_rows = panel_index * row_tiles + jnp.arange(row_tiles, dtype=jnp.int32)
    first_column = (column_group - own_rows) % groups
    own_resid = resid.reshape(row_tiles, tile_size, local_samples)
    own_data = samples.reshape(row_tiles, tile_size, local_samples)
    all_resid, all_data = (
        lax.all_gather(resid, "wide", axis=0, tiled=True),
        lax.all_gather(samples, "wide", axis=0, tiled=True),
    )
    resid_tiles = all_resid.reshape(tiles, tile_size, local_samples)
    data_tiles = all_data.reshape(tiles, tile_size, local_samples)
    positions = jnp.arange(per_class * lax.axis_size("blk"), dtype=jnp.int32)
    classes = positions // per_class
    within = positions % per_class
    column_ids = (classes[:, None] - own_rows[None, :]) % groups + groups * within[:, None]
    forward = jnp.einsum(
        "kis,pkjs->pkij", own_resid, data_tiles[column_ids], preferred_element_type=jnp.float32
    )
    backward = jnp.einsum(
        "kis,pkjs->pkij", own_data, resid_tiles[column_ids], preferred_element_type=jnp.float32
    )
    summed = (
        lax.psum_scatter(0.5 * (forward + backward), "blk", scatter_dimension=0, tiled=True)
        / total_samples
    )
    precision_tiles = precision[:, 0]
    active_flags = active[:, 0].astype(jnp.float32)
    gradient_part = summed.transpose(1, 0, 2, 3)
    column_ids = first_column[:, None] + groups * jnp.arange(per_class, dtype=jnp.int32)[None, :]
    same_tile = column_ids == own_rows[:, None]
    identity = jnp.eye(tile_size, dtype=bool)
    on_diag = same_tile[:, :, None, None] & identity
    inverse = jnp.where(on_diag, 1.0 / jnp.where(on_diag, precision_tiles, 1.0), 0.0)
    stepped = precision_tiles - STEP * (gradient_part + RIDGE * precision_tiles - inverse)
    shrunk = jnp.sign(stepped) * jnp.maximum(jnp.abs(stepped) - STEP * LASSO, 0.0)
    updated = jnp.where(on_diag, stepped, shrunk) * active_flags[:, :, None, None]
    return updated[:, None]


MESH = pl.DeviceIdType.MESH


def pick(table, i):
    value = jnp.int32(table[0])
    for n in range(1, len(table)):
        value = jnp.where(i == n, jnp.int32(table[n]), value)
    return value


def kernel(
    depth, scale, resid, samples, weights, flags, out,
    own, cols, held, stage, landed, recv, own_recv, res_recv, send, res_send, fill, out_sem,
):
    b = lax.axis_index("blk")
    w = lax.axis_index("wide")
    nb = 1 - b
    z, y, c = w // 4, (w // 2) % 2, w % 2
    per = own.shape[3]
    tile = own.shape[4]
    panels = cols.shape[1]
    up, down = (z + 1 < depth), (z > 0)

    def at(zz, yy, cc):
        return (zz * 2 + yy) * 2 + cc

    orders = [sorted((o for o in range(depth) if o != i), key=lambda o: (abs(o - i), o)) for i in range(depth)]

    def order(k):
        value = z
        for n in range(1, depth):
            value = jnp.where(k == n, pick([orders[i][n - 1] for i in range(depth)], z), value)
        return value

    loads = []
    for a, src in enumerate((resid, samples)):
        for p in range(2):
            loads.append(pltpu.make_async_copy(src.at[:, p], own.at[b, p, a], fill.at[2 * a + p]))
    for load in loads:
        load.start()
    load_weights = pltpu.make_async_copy(weights, held, fill.at[4])
    load_weights.start()

    barrier = pltpu.get_barrier_semaphore()

    def greet(**device):
        pl.semaphore_signal(barrier, inc=1, device_id=device, device_id_type=MESH)

    greet(blk=nb)
    greet(wide=at(z, 1 - y, c))
    greet(wide=at(z, y, 1 - c))

    @pl.when(up)
    def _():
        greet(wide=at(z + 1, y, c))

    @pl.when(down)
    def _():
        greet(wide=at(z - 1, y, c))

    pl.semaphore_wait(barrier, 3 + jnp.where(up, 1, 0) + jnp.where(down, 1, 0))

    def push(h, src, panel, k, lane, target):
        return pltpu.make_async_remote_copy(
            src_ref=src, dst_ref=cols.at[h, panel], send_sem=send.at[h, k, lane],
            recv_sem=recv.at[h, panel], device_id={"wide": target}, device_id_type=MESH,
        )

    def arrive(h, panel):
        push(h, cols.at[h, panel], panel, 0, 0, at(z, 1 - y, c)).wait_recv()

    def own_pushes(h):
        src = own.at[h, b]
        return (
            (up, push(h, src, w, 0, 0, at(z + 1, y, c))),
            (down, push(h, src, w, 0, 1, at(z - 1, y, c))),
            (None, push(h, src, w, 0, 2, at(z, 1 - y, c))),
            (None, push(h, src, w, 0, 3, at(z, y, 1 - c))),
        )

    def z_pushes(h, k):
        zk = order(k)
        panel = at(zk, y, c)
        src = cols.at[h, panel]
        onward = jnp.where(zk < z, z + 1, z - 1)
        exists = jnp.logical_and(onward >= 0, onward < depth)
        return (
            (exists, push(h, src, panel, k, 0, at(onward, y, c))),
            (None, push(h, src, panel, k, 2, at(z, 1 - y, c))),
            (None, push(h, src, panel, k, 3, at(z, y, 1 - c))),
        )

    def y_push(h, k):
        panel = at(order(k), 1 - y, c)
        return ((None, push(h, cols.at[h, panel], panel, k, 4, at(z, y, 1 - c))),)

    def start(pushes):
        for when, copy in pushes:
            if when is None:
                copy.start()
            else:
                pl.when(when)(copy.start)

    def drain(pushes):
        for when, copy in pushes:
            if when is None:
                copy.wait_send()
            else:
                pl.when(when)(copy.wait_send)

    def forward_z(k):
        for h in (b, nb):
            arrive(h, at(order(k), y, c))
            start(z_pushes(h, k))

    def swap(i):
        p = nb if i == 0 else b
        return pltpu.make_async_remote_copy(
            src_ref=own.at[b, p], dst_ref=own.at[b, p], send_sem=res_send.at[panels + i],
            recv_sem=own_recv.at[i], device_id={"blk": nb}, device_id_type=MESH,
        )

    def hand(panel):
        return pltpu.make_async_remote_copy(
            src_ref=stage.at[panel], dst_ref=landed.at[panel], send_sem=res_send.at[panel],
            recv_sem=res_recv.at[panel], device_id={"blk": nb}, device_id_type=MESH,
        )

    def store(p, panel):
        span = pl.ds(panel * per, per)
        return pltpu.make_async_copy(
            held.at[:, p, span], out.at[:, p, span], out_sem.at[p, panel]
        )

    def gram(p, side):
        total = None
        for h in range(2):
            for a in range(2):
                left = own[h, p, a].reshape(per * tile, -1)
                right = side(h, 1 - a).reshape(per * tile, -1)
                part = lax.dot_general(
                    left, right, (((1,), (1,)), ((), ())), preferred_element_type=jnp.float32
                )
                total = part if total is None else total + part
        return total * scale

    def finish(p, panel, part, diagonal):
        for t in range(per):
            for u in range(per):
                slot = panel * per + u
                weight = held[t, p, slot]
                half = part(t, u) + RIDGE * weight
                if diagonal and t == u:
                    rows = lax.broadcasted_iota(jnp.int32, (tile, tile), 0)
                    columns = lax.broadcasted_iota(jnp.int32, (tile, tile), 1)
                    on_diag = rows == columns + b * (2 * tile)
                    inverse = jnp.where(on_diag, 1.0 / jnp.where(on_diag, weight, 1.0), 0.0)
                    stepped = weight - STEP * (half - inverse)
                else:
                    stepped = weight - STEP * half
                bound = STEP * LASSO
                updated = stepped - jnp.clip(stepped, -bound, bound)
                if diagonal and t == u:
                    updated = jnp.where(on_diag, stepped, updated)
                flag = flags[2 * t + p, slot].astype(jnp.float32)
                held[t, p, slot] = updated * flag
        store(p, panel).start()

    for load in loads:
        load.wait()
    for i in range(2):
        swap(i).start()
    start(own_pushes(b))
    swap_in = [
        pltpu.make_async_remote_copy(
            src_ref=own.at[nb, p], dst_ref=own.at[nb, p], send_sem=res_send.at[panels + i],
            recv_sem=own_recv.at[i], device_id={"blk": nb}, device_id_type=MESH,
        )
        for i, p in enumerate((b, nb))
    ]
    swap_in[0].wait_recv()
    start(own_pushes(nb))
    swap_in[1].wait_recv()
    forward_z(1)
    load_weights.wait()

    for p in range(2):
        parity = b if p == 0 else nb
        total = gram(p, lambda h, a: own[h, parity, a])
        finish(p, w, lambda t, u: total[t * tile:(t + 1) * tile, u * tile:(u + 1) * tile], True)

    def place(s):
        k, i = s // 4, s % 4
        yy = jnp.where(i < 2, y, 1 - y)
        cc = jnp.where(i % 2 == 0, c, 1 - c)
        return k, i, at(order(k), yy, cc)

    def compute(s, carry):
        k, i, panel = place(s)

        @pl.when(jnp.logical_and(i == 2, jnp.logical_and(k > 0, k < depth - 1)))
        def _():
            forward_z(k + 1)

        @pl.when(i != 0)
        def _():
            for h in (b, nb):
                arrive(h, panel)

        @pl.when(i == 2)
        def _():
            for h in (b, nb):
                start(y_push(h, k))

        total = gram(1, lambda h, a: cols[h, panel, a])
        for t in range(per):
            for u in range(per):
                stage[panel, t, u] = total[t * tile:(t + 1) * tile, u * tile:(u + 1) * tile]
        hand(panel).start()
        kept = gram(0, lambda h, a: cols[h, panel, a])
        finish(0, panel, lambda t, u: kept[t * tile:(t + 1) * tile, u * tile:(u + 1) * tile], False)
        return carry

    lax.fori_loop(1, 4 * depth, compute, 0)

    def receive(s, carry):
        panel = place(s)[2]
        hand(panel).wait_recv()
        finish(1, panel, lambda t, u: landed[panel, t, u], False)
        return carry

    lax.fori_loop(1, 4 * depth, receive, 0)

    for i in range(2):
        swap(i).wait_send()
    for h in (b, nb):
        drain(own_pushes(h))

    def drain_group(k, carry):
        for h in (b, nb):
            drain(y_push(h, k))

            @pl.when(k > 0)
            def _():
                drain(z_pushes(h, k))
        return carry

    lax.fori_loop(0, depth, drain_group, 0)

    def drain_panel(s, carry):
        panel = place(s)[2]
        hand(panel).wait_send()
        for p in range(2):
            store(p, panel).wait()
        return carry

    lax.fori_loop(1, 4 * depth, drain_panel, 0)
    for p in range(2):
        store(p, w).wait()


def ring(resid, samples, precision, active):
    panels = lax.axis_size("wide")
    row_tiles, _, per_class, tile, _ = precision.shape
    per = row_tiles // 2
    half = resid.shape[1]
    depth = panels // 4
    scale = 0.5 / (2 * half)
    any_spec = pl.BlockSpec(memory_space=pl.ANY)
    bf16, f32 = resid.dtype, jnp.float32
    dma = pltpu.SemaphoreType.DMA
    updated = pl.pallas_call(
        functools.partial(kernel, depth, scale),
        out_shape=jax.ShapeDtypeStruct((per, 2, per_class, tile, tile), f32),
        in_specs=[any_spec, any_spec, any_spec, pl.BlockSpec(memory_space=pltpu.SMEM)],
        out_specs=any_spec,
        scratch_shapes=[
            pltpu.VMEM((2, 2, 2, per, tile, half), bf16),
            pltpu.VMEM((2, panels, 2, per, tile, half), bf16),
            pltpu.VMEM((per, 2, per_class, tile, tile), f32),
            pltpu.VMEM((panels, per, per, tile, tile), f32),
            pltpu.VMEM((panels, per, per, tile, tile), f32),
            dma((2, panels)),
            dma((2,)),
            dma((panels,)),
            dma((2, depth, 5)),
            dma((panels + 2,)),
            dma((5,)),
            dma((2, panels)),
        ],
        compiler_params=pltpu.CompilerParams(
            collective_id=0, has_side_effects=True, vmem_limit_bytes=60 * 1024 * 1024
        ),
    )(
        resid.reshape(per, 2, tile, half),
        samples.reshape(per, 2, tile, half),
        precision.reshape(per, 2, per_class, tile, tile),
        active[:, 0],
    )
    return updated.reshape(precision.shape)


def body(resid, samples, precision, active):
    panels = lax.axis_size("wide")
    row_tiles, _, per_class, tile, _ = precision.shape
    words = 8 * per_class * row_tiles * tile * tile + 4 * panels * row_tiles * tile * resid.shape[1]
    if lax.axis_size("blk") == 2 and panels % 4 == 0 and row_tiles % 2 == 0 and words < 52 * 1024 * 1024:
        return ring(resid, samples, precision, active)
    return local(resid, samples, precision, active)


def solution(mesh):
    in_specs = (
        P("wide", "blk"),
        P("wide", "blk"),
        P("wide", "blk", None, None, None),
        P("wide", "blk", None),
    )
    out_specs = P("wide", "blk", None, None, None)
    return jax.shard_map(body, mesh=mesh, in_specs=in_specs, out_specs=out_specs, check_vma=False)
```

```python
import functools

import jax
import jax.numpy as jnp
from jax import lax
from jax.experimental import pallas as pl
from jax.experimental.pallas import tpu as pltpu
from jax.sharding import PartitionSpec as P

STEP = 1.0
LASSO = 0.1
RIDGE = 0.5


def local(resid, samples, precision, active):
    groups = lax.axis_size("blk")
    column_group = lax.axis_index("blk")
    panel_index = lax.axis_index("wide")
    row_tiles = precision.shape[0]
    per_class = precision.shape[2]
    tile_size = precision.shape[3]
    tiles = per_class * groups
    local_samples = resid.shape[1]
    total_samples = local_samples * groups
    own_rows = panel_index * row_tiles + jnp.arange(row_tiles, dtype=jnp.int32)
    first_column = (column_group - own_rows) % groups
    own_resid = resid.reshape(row_tiles, tile_size, local_samples)
    own_data = samples.reshape(row_tiles, tile_size, local_samples)
    all_resid, all_data = (
        lax.all_gather(resid, "wide", axis=0, tiled=True),
        lax.all_gather(samples, "wide", axis=0, tiled=True),
    )
    resid_tiles = all_resid.reshape(tiles, tile_size, local_samples)
    data_tiles = all_data.reshape(tiles, tile_size, local_samples)
    positions = jnp.arange(per_class * lax.axis_size("blk"), dtype=jnp.int32)
    classes = positions // per_class
    within = positions % per_class
    column_ids = (classes[:, None] - own_rows[None, :]) % groups + groups * within[:, None]
    forward = jnp.einsum(
        "kis,pkjs->pkij", own_resid, data_tiles[column_ids], preferred_element_type=jnp.float32
    )
    backward = jnp.einsum(
        "kis,pkjs->pkij", own_data, resid_tiles[column_ids], preferred_element_type=jnp.float32
    )
    summed = (
        lax.psum_scatter(0.5 * (forward + backward), "blk", scatter_dimension=0, tiled=True)
        / total_samples
    )
    precision_tiles = precision[:, 0]
    active_flags = active[:, 0].astype(jnp.float32)
    gradient_part = summed.transpose(1, 0, 2, 3)
    column_ids = first_column[:, None] + groups * jnp.arange(per_class, dtype=jnp.int32)[None, :]
    same_tile = column_ids == own_rows[:, None]
    identity = jnp.eye(tile_size, dtype=bool)
    on_diag = same_tile[:, :, None, None] & identity
    inverse = jnp.where(on_diag, 1.0 / jnp.where(on_diag, precision_tiles, 1.0), 0.0)
    stepped = precision_tiles - STEP * (gradient_part + RIDGE * precision_tiles - inverse)
    shrunk = jnp.sign(stepped) * jnp.maximum(jnp.abs(stepped) - STEP * LASSO, 0.0)
    updated = jnp.where(on_diag, stepped, shrunk) * active_flags[:, :, None, None]
    return updated[:, None]


MESH = pl.DeviceIdType.MESH


def pick(table, i):
    value = jnp.int32(table[0])
    for n in range(1, len(table)):
        value = jnp.where(i == n, jnp.int32(table[n]), value)
    return value


def kernel(
    depth, scale, resid, samples, weights, flags, held,
    own, cols, mate, stage, landed, recv, own_recv, res_recv, mate_recv, send, res_send, fill,
):
    b = lax.axis_index("blk")
    w = lax.axis_index("wide")
    nb = 1 - b
    z, y, c = w // 4, (w // 2) % 2, w % 2
    per = own.shape[3]
    tile = own.shape[4]
    panels = cols.shape[1]
    up, down = (z + 1 < depth), (z > 0)

    def at(zz, yy, cc):
        return (zz * 2 + yy) * 2 + cc

    orders = [sorted((o for o in range(depth) if o != i), key=lambda o: (abs(o - i), o)) for i in range(depth)]
    inner = pick([int(len(o) > 1 and abs(o[1] - i) == 1) for i, o in enumerate(orders)], z)

    def order(k):
        value = z
        for n in range(1, depth):
            value = jnp.where(k == n, pick([orders[i][n - 1] for i in range(depth)], z), value)
        return value

    loads = []
    for a, src in enumerate((resid, samples)):
        for p in range(2):
            loads.append(pltpu.make_async_copy(src.at[:, p], own.at[b, p, a], fill.at[2 * a + p]))
    for load in loads:
        load.start()
    load_weights = pltpu.make_async_copy(weights, held, fill.at[4])
    load_weights.start()

    barrier = pltpu.get_barrier_semaphore()

    def greet(**device):
        pl.semaphore_signal(barrier, inc=1, device_id=device, device_id_type=MESH)

    greet(blk=nb)
    greet(wide=at(z, 1 - y, c))
    greet(wide=at(z, y, 1 - c))

    @pl.when(up)
    def _():
        greet(wide=at(z + 1, y, c))

    @pl.when(down)
    def _():
        greet(wide=at(z - 1, y, c))

    pl.semaphore_wait(barrier, 3 + jnp.where(up, 1, 0) + jnp.where(down, 1, 0))

    def push(h, src, panel, k, lane, target):
        return pltpu.make_async_remote_copy(
            src_ref=src, dst_ref=cols.at[h, panel], send_sem=send.at[h, k, lane],
            recv_sem=recv.at[h, panel], device_id={"wide": target}, device_id_type=MESH,
        )

    def arrive(h, panel):
        push(h, cols.at[h, panel], panel, 0, 0, at(z, 1 - y, c)).wait_recv()

    def own_pushes(h):
        src = own.at[h, b]
        return (
            (up, push(h, src, w, 0, 0, at(z + 1, y, c))),
            (down, push(h, src, w, 0, 1, at(z - 1, y, c))),
            (None, push(h, src, w, 0, 2, at(z, 1 - y, c))),
            (None, push(h, src, w, 0, 3, at(z, y, 1 - c))),
        )

    def mate_push(h):
        return pltpu.make_async_remote_copy(
            src_ref=own.at[h, nb], dst_ref=mate.at[h], send_sem=send.at[h, 0, 5],
            recv_sem=mate_recv.at[h], device_id={"wide": at(z, y, 1 - c)}, device_id_type=MESH,
        )

    def z_pushes(h, k):
        zk = order(k)
        panel = at(zk, y, c)
        src = cols.at[h, panel]
        onward = jnp.where(zk < z, z + 1, z - 1)
        exists = jnp.logical_and(onward >= 0, onward < depth)
        return (
            (exists, push(h, src, panel, k, 0, at(onward, y, c))),
            (None, push(h, src, panel, k, 2, at(z, 1 - y, c))),
            (None, push(h, src, panel, k, 3, at(z, y, 1 - c))),
        )

    def y_push(h, k):
        panel = at(order(k), 1 - y, c)
        return ((None, push(h, cols.at[h, panel], panel, k, 4, at(z, y, 1 - c))),)

    def start(pushes):
        for when, copy in pushes:
            if when is None:
                copy.start()
            else:
                pl.when(when)(copy.start)

    def drain(pushes):
        for when, copy in pushes:
            if when is None:
                copy.wait_send()
            else:
                pl.when(when)(copy.wait_send)

    def forward_z(k):
        for h in (b, nb):
            arrive(h, at(order(k), y, c))
            start(z_pushes(h, k))

    def swap(i):
        p = nb if i == 0 else b
        return pltpu.make_async_remote_copy(
            src_ref=own.at[b, p], dst_ref=own.at[b, p], send_sem=res_send.at[panels + i],
            recv_sem=own_recv.at[i], device_id={"blk": nb}, device_id_type=MESH,
        )

    def hand(panel):
        return pltpu.make_async_remote_copy(
            src_ref=stage.at[panel], dst_ref=landed.at[panel], send_sem=res_send.at[panel],
            recv_sem=res_recv.at[panel], device_id={"blk": nb}, device_id_type=MESH,
        )

    def gram(p, side):
        total = None
        for h in range(2):
            for a in range(2):
                left = own[h, p, a].reshape(per * tile, -1)
                right = side(h, 1 - a).reshape(per * tile, -1)
                part = lax.dot_general(
                    left, right, (((1,), (1,)), ((), ())), preferred_element_type=jnp.float32
                )
                total = part if total is None else total + part
        return total * scale

    def finish(p, panel, part, diagonal):
        for t in range(per):
            for u in range(per):
                slot = panel * per + u
                weight = held[t, p, slot]
                half = part(t, u) + RIDGE * weight
                if diagonal and t == u:
                    rows = lax.broadcasted_iota(jnp.int32, (tile, tile), 0)
                    columns = lax.broadcasted_iota(jnp.int32, (tile, tile), 1)
                    on_diag = rows == columns + b * (2 * tile)
                    inverse = jnp.where(on_diag, 1.0 / jnp.where(on_diag, weight, 1.0), 0.0)
                    stepped = weight - STEP * (half - inverse)
                else:
                    stepped = weight - STEP * half
                bound = STEP * LASSO
                updated = stepped - jnp.clip(stepped, -bound, bound)
                if diagonal and t == u:
                    updated = jnp.where(on_diag, stepped, updated)
                flag = flags[2 * t + p, slot].astype(jnp.float32)
                held[t, p, slot] = updated * flag

    for load in loads:
        load.wait()
    for i in range(2):
        swap(i).start()
    start(own_pushes(b))
    mate_push(b).start()
    swap_in = [
        pltpu.make_async_remote_copy(
            src_ref=own.at[nb, p], dst_ref=own.at[nb, p], send_sem=res_send.at[panels + i],
            recv_sem=own_recv.at[i], device_id={"blk": nb}, device_id_type=MESH,
        )
        for i, p in enumerate((b, nb))
    ]
    swap_in[0].wait_recv()
    start(own_pushes(nb))
    swap_in[1].wait_recv()
    forward_z(1)

    def place(s):
        k, i = s // 4, s % 4
        yy = jnp.where(i < 2, y, 1 - y)
        cc = jnp.where(i % 2 == 0, c, 1 - c)
        return k, i, at(order(k), yy, cc)

    def cut(total):
        return lambda t, u: total[t * tile:(t + 1) * tile, u * tile:(u + 1) * tile]

    def compute(s, carry):
        k, i, panel = place(s)
        ahead = k + 1 + inner

        @pl.when(jnp.logical_and(i == 2, jnp.logical_and(ahead > 1, ahead < depth)))
        def _():
            forward_z(ahead)

        @pl.when(i != 0)
        def _():
            for h in (b, nb):
                arrive(h, panel)

        @pl.when(i == 2)
        def _():
            for h in (b, nb):
                start(y_push(h, k))

        total = cut(gram(1, lambda h, a: cols[h, panel, a]))
        for t in range(per):
            for u in range(per):
                stage[panel, t, u] = total(t, u)
        hand(panel).start()

        @pl.when(s == 2)
        def _():
            mate_push(nb).start()
            load_weights.wait()

        finish(0, panel, cut(gram(0, lambda h, a: cols[h, panel, a])), False)
        return carry

    lax.fori_loop(2, 4 * depth, compute, 0)

    for p in range(2):
        parity = b if p == 0 else nb
        finish(p, w, cut(gram(p, lambda h, a: own[h, parity, a])), True)
    beside = at(z, y, 1 - c)
    for h in (b, nb):
        arrive(h, beside)
        mate_push(h).wait_recv()
    finish(0, beside, cut(gram(0, lambda h, a: cols[h, beside, a])), False)
    finish(1, beside, cut(gram(1, lambda h, a: mate[h, a])), False)

    def receive(s, carry):
        panel = place(s)[2]
        hand(panel).wait_recv()
        finish(1, panel, lambda t, u: landed[panel, t, u], False)
        return carry

    lax.fori_loop(2, 4 * depth, receive, 0)

    for i in range(2):
        swap(i).wait_send()
    for h in (b, nb):
        drain(own_pushes(h))
        mate_push(h).wait_send()

    def drain_group(k, carry):
        for h in (b, nb):
            drain(y_push(h, k))

            @pl.when(k > 0)
            def _():
                drain(z_pushes(h, k))
        return carry

    lax.fori_loop(0, depth, drain_group, 0)

    def drain_panel(s, carry):
        hand(place(s)[2]).wait_send()
        return carry

    lax.fori_loop(2, 4 * depth, drain_panel, 0)


def ring(resid, samples, precision, active):
    panels = lax.axis_size("wide")
    row_tiles, _, per_class, tile, _ = precision.shape
    per = row_tiles // 2
    half = resid.shape[1]
    depth = panels // 4
    scale = 0.5 / (2 * half)
    any_spec = pl.BlockSpec(memory_space=pl.ANY)
    bf16, f32 = resid.dtype, jnp.float32
    dma = pltpu.SemaphoreType.DMA
    updated = pl.pallas_call(
        functools.partial(kernel, depth, scale),
        out_shape=pltpu.VMEM((per, 2, per_class, tile, tile), f32),
        in_specs=[any_spec, any_spec, any_spec, pl.BlockSpec(memory_space=pltpu.SMEM)],
        out_specs=pl.BlockSpec(memory_space=pltpu.VMEM),
        scratch_shapes=[
            pltpu.VMEM((2, 2, 2, per, tile, half), bf16),
            pltpu.VMEM((2, panels, 2, per, tile, half), bf16),
            pltpu.VMEM((2, 2, per, tile, half), bf16),
            pltpu.VMEM((panels, per, per, tile, tile), f32),
            pltpu.VMEM((panels, per, per, tile, tile), f32),
            dma((2, panels)),
            dma((2,)),
            dma((panels,)),
            dma((2,)),
            dma((2, depth, 6)),
            dma((panels + 2,)),
            dma((5,)),
        ],
        compiler_params=pltpu.CompilerParams(
            collective_id=0, has_side_effects=True, vmem_limit_bytes=52 * 1024 * 1024
        ),
    )(
        resid.reshape(per, 2, tile, half),
        samples.reshape(per, 2, tile, half),
        precision.reshape(per, 2, per_class, tile, tile),
        active[:, 0],
    )
    return updated.reshape(precision.shape)


def body(resid, samples, precision, active):
    panels = lax.axis_size("wide")
    row_tiles, _, per_class, tile, _ = precision.shape
    words = 8 * per_class * row_tiles * tile * tile + 4 * panels * row_tiles * tile * resid.shape[1]
    if lax.axis_size("blk") == 2 and panels % 4 == 0 and row_tiles % 2 == 0 and words < 52 * 1024 * 1024:
        return ring(resid, samples, precision, active)
    return local(resid, samples, precision, active)


def solution(mesh):
    in_specs = (
        P("wide", "blk"),
        P("wide", "blk"),
        P("wide", "blk", None, None, None),
        P("wide", "blk", None),
    )
    out_specs = P("wide", "blk", None, None, None)
    return jax.shard_map(body, mesh=mesh, in_specs=in_specs, out_specs=out_specs, check_vma=False)
```

```python
import functools

import jax
import jax.numpy as jnp
from jax import lax
from jax.experimental import pallas as pl
from jax.experimental.pallas import tpu as pltpu
from jax.sharding import PartitionSpec as P

STEP = 1.0
LASSO = 0.1
RIDGE = 0.5


def local(resid, samples, precision, active):
    groups = lax.axis_size("blk")
    column_group = lax.axis_index("blk")
    panel_index = lax.axis_index("wide")
    row_tiles = precision.shape[0]
    per_class = precision.shape[2]
    tile_size = precision.shape[3]
    tiles = per_class * groups
    local_samples = resid.shape[1]
    total_samples = local_samples * groups
    own_rows = panel_index * row_tiles + jnp.arange(row_tiles, dtype=jnp.int32)
    first_column = (column_group - own_rows) % groups
    own_resid = resid.reshape(row_tiles, tile_size, local_samples)
    own_data = samples.reshape(row_tiles, tile_size, local_samples)
    all_resid, all_data = (
        lax.all_gather(resid, "wide", axis=0, tiled=True),
        lax.all_gather(samples, "wide", axis=0, tiled=True),
    )
    resid_tiles = all_resid.reshape(tiles, tile_size, local_samples)
    data_tiles = all_data.reshape(tiles, tile_size, local_samples)
    positions = jnp.arange(per_class * lax.axis_size("blk"), dtype=jnp.int32)
    classes = positions // per_class
    within = positions % per_class
    column_ids = (classes[:, None] - own_rows[None, :]) % groups + groups * within[:, None]
    forward = jnp.einsum(
        "kis,pkjs->pkij", own_resid, data_tiles[column_ids], preferred_element_type=jnp.float32
    )
    backward = jnp.einsum(
        "kis,pkjs->pkij", own_data, resid_tiles[column_ids], preferred_element_type=jnp.float32
    )
    summed = (
        lax.psum_scatter(0.5 * (forward + backward), "blk", scatter_dimension=0, tiled=True)
        / total_samples
    )
    precision_tiles = precision[:, 0]
    active_flags = active[:, 0].astype(jnp.float32)
    gradient_part = summed.transpose(1, 0, 2, 3)
    column_ids = first_column[:, None] + groups * jnp.arange(per_class, dtype=jnp.int32)[None, :]
    same_tile = column_ids == own_rows[:, None]
    identity = jnp.eye(tile_size, dtype=bool)
    on_diag = same_tile[:, :, None, None] & identity
    inverse = jnp.where(on_diag, 1.0 / jnp.where(on_diag, precision_tiles, 1.0), 0.0)
    stepped = precision_tiles - STEP * (gradient_part + RIDGE * precision_tiles - inverse)
    shrunk = jnp.sign(stepped) * jnp.maximum(jnp.abs(stepped) - STEP * LASSO, 0.0)
    updated = jnp.where(on_diag, stepped, shrunk) * active_flags[:, :, None, None]
    return updated[:, None]


MESH = pl.DeviceIdType.MESH


def pick(table, i):
    value = jnp.int32(table[0])
    for n in range(1, len(table)):
        value = jnp.where(i == n, jnp.int32(table[n]), value)
    return value


def kernel(
    depth, scale, resid, samples, weights, flags, held,
    own, cols, mate, stage, landed, recv, own_recv, res_recv, mate_recv, send, own_send, res_send,
    mate_send, fill,
):
    b = lax.axis_index("blk")
    w = lax.axis_index("wide")
    nb = 1 - b
    z, y, c = w // 4, (w // 2) % 2, w % 2
    per = own.shape[2]
    tile = own.shape[4]
    panels = cols.shape[1]
    up, down = (z + 1 < depth), (z > 0)
    last = depth - 1
    inner = jnp.where(up, 1, 0) * jnp.where(down, 1, 0)
    far = jnp.where(2 * z < depth, 1, 0)
    far_z = far * last

    def at(zz, yy, cc):
        return (zz * 2 + yy) * 2 + cc

    orders = [
        sorted((o for o in range(depth) if o != i), key=lambda o: (abs(o - i), o))
        for i in range(depth)
    ]

    def order(k):
        value = z
        for n in range(1, depth):
            value = jnp.where(k == n, pick([orders[i][n - 1] for i in range(depth)], z), value)
        return value

    loads = []
    for a, src in enumerate((resid, samples)):
        for p in range(2):
            loads.append(
                pltpu.make_async_copy(src.at[:, p], own.at[b, p, :, a], fill.at[2 * a + p])
            )
    for load in loads:
        load.start()
    load_weights = pltpu.make_async_copy(weights, held, fill.at[4])

    barrier = pltpu.get_barrier_semaphore()

    def greet(**device):
        pl.semaphore_signal(barrier, inc=1, device_id=device, device_id_type=MESH)

    greet(blk=nb)
    greet(wide=at(z, 1 - y, c))
    greet(wide=at(z, y, 1 - c))

    @pl.when(up)
    def _():
        greet(wide=at(z + 1, y, c))

    @pl.when(down)
    def _():
        greet(wide=at(z - 1, y, c))

    pl.semaphore_wait(barrier, 3 + jnp.where(up, 1, 0) + jnp.where(down, 1, 0))

    def push(h, t, src, panel, k, lane, target):
        return pltpu.make_async_remote_copy(
            src_ref=src, dst_ref=cols.at[h, panel, t], send_sem=send.at[h, t, k, lane],
            recv_sem=recv.at[h, panel, t], device_id={"wide": target}, device_id_type=MESH,
        )

    def arrive(h, t, panel):
        push(h, t, cols.at[h, panel, t], panel, 0, 0, at(z, 1 - y, c)).wait_recv()

    def own_pushes(h, t):
        src = own.at[h, b, t]
        return (
            (up, push(h, t, src, w, 0, 0, at(z + 1, y, c))),
            (down, push(h, t, src, w, 0, 1, at(z - 1, y, c))),
            (None, push(h, t, src, w, 0, 2, at(z, 1 - y, c))),
            (None, push(h, t, src, w, 0, 3, at(z, y, 1 - c))),
        )

    def z_pushes(h, t, k):
        zk = order(k)
        panel = at(zk, y, c)
        src = cols.at[h, panel, t]
        onward = jnp.where(zk < z, z + 1, z - 1)
        exists = jnp.logical_and(onward >= 0, onward < depth)
        return (
            (exists, push(h, t, src, panel, k, 0, at(onward, y, c))),
            (None, push(h, t, src, panel, k, 2, at(z, 1 - y, c))),
            (None, push(h, t, src, panel, k, 3, at(z, y, 1 - c))),
        )

    def y_push(h, t, k):
        panel = at(order(k), 1 - y, c)
        return ((None, push(h, t, cols.at[h, panel, t], panel, k, 4, at(z, y, 1 - c))),)

    def mate_push(h, src, slot, lane, target):
        return pltpu.make_async_remote_copy(
            src_ref=src, dst_ref=mate.at[h, slot], send_sem=mate_send.at[h, lane],
            recv_sem=mate_recv.at[h, slot], device_id={"wide": target}, device_id_type=MESH,
        )

    def beside_push(h):
        return ((None, mate_push(h, own.at[h, nb], 0, 0, at(z, y, 1 - c))),)

    def end_push(h):
        slot = jnp.where(z == 0, 1, 2)
        inward = jnp.where(z == 0, z + 1, z - 1)
        return ((inner == 0, mate_push(h, own.at[h, nb], slot, 1, at(inward, y, c))),)

    def relay_push(h, end, lane):
        onward = jnp.where(end == 0, z + 1, z - 1)
        return ((inner == 1, mate_push(h, mate.at[h, 1 + end], 1 + end, lane, at(onward, y, c))),)

    def far_push(h):
        return ((None, mate_push(h, mate.at[h, 1 + far], 3, 4, at(z, y, 1 - c))),)

    def mate_arrive(h, slot):
        mate_push(h, mate.at[h, slot], slot, 0, at(z, y, 1 - c)).wait_recv()

    def start(pushes):
        for when, copy in pushes:
            if when is None:
                copy.start()
            else:
                pl.when(when)(copy.start)

    def drain(pushes):
        for when, copy in pushes:
            if when is None:
                copy.wait_send()
            else:
                pl.when(when)(copy.wait_send)

    def forward_z(k):
        for t in range(per):
            for h in (b, nb):
                arrive(h, t, at(order(k), y, c))
                start(z_pushes(h, t, k))

    def relay_near(h):
        @pl.when(inner == 1)
        def _():
            mate_arrive(h, 2 - far)
            start(relay_push(h, 1 - far, 2))

    def relay_far(h):
        mate_arrive(h, 1 + far)
        start(relay_push(h, far, 3))
        start(far_push(h))

    def swap(h, i, t):
        p = (nb, b)[i] if h is b else (b, nb)[i]
        return pltpu.make_async_remote_copy(
            src_ref=own.at[h, p, t], dst_ref=own.at[h, p, t], send_sem=own_send.at[i, t],
            recv_sem=own_recv.at[i, t], device_id={"blk": nb}, device_id_type=MESH,
        )

    def hand(panel, u):
        return pltpu.make_async_remote_copy(
            src_ref=stage.at[panel, u], dst_ref=landed.at[panel, u],
            send_sem=res_send.at[panel, u], recv_sem=res_recv.at[panel, u],
            device_id={"blk": nb}, device_id_type=MESH,
        )

    def gram(p, side):
        total = None
        for h in range(2):
            for a in range(2):
                left = own[h, p, :, a].reshape(per * tile, -1)
                right = side(h, 1 - a)
                part = lax.dot_general(
                    left, right, (((1,), (1,)), ((), ())), preferred_element_type=jnp.float32
                )
                total = part if total is None else total + part
        return total * scale

    def finish(p, panel, u, part, diagonal):
        for t in range(per):
            slot = panel * per + u
            weight = held[t, p, slot]
            half = part(t) + RIDGE * weight
            if diagonal and t == u:
                rows = lax.broadcasted_iota(jnp.int32, (tile, tile), 0)
                columns = lax.broadcasted_iota(jnp.int32, (tile, tile), 1)
                on_diag = rows == columns + b * (2 * tile)
                inverse = jnp.where(on_diag, 1.0 / jnp.where(on_diag, weight, 1.0), 0.0)
                stepped = weight - STEP * (half - inverse)
            else:
                stepped = weight - STEP * half
            bound = STEP * LASSO
            updated = stepped - jnp.clip(stepped, -bound, bound)
            if diagonal and t == u:
                updated = jnp.where(on_diag, stepped, updated)
            flag = flags[2 * t + p, slot].astype(jnp.float32)
            held[t, p, slot] = updated * flag

    def cut(total):
        return lambda t: total[t * tile:(t + 1) * tile]

    for load in loads:
        load.wait()
    for i in range(2):
        for t in range(per):
            swap(b, i, t).start()
    for t in range(per):
        start(own_pushes(b, t))
    load_weights.start()
    for t in range(per):
        swap(nb, 0, t).wait_recv()
        start(own_pushes(nb, t))
    start(end_push(b))
    start(beside_push(b))
    for h in (b, nb):
        for t in range(per):
            arrive(h, t, at(order(1), y, c))
            start(z_pushes(h, t, 1))
    for t in range(per):
        swap(nb, 1, t).wait_recv()
    start(end_push(nb))
    load_weights.wait()

    def place(n):
        s = n + 2 + jnp.where(n < 4 * depth - 6, 0, 2)
        k, i = s // 4, s % 4
        yy = jnp.where(i < 2, y, 1 - y)
        cc = jnp.where(i % 2 == 0, c, 1 - c)
        return k, i, at(order(k), yy, cc)

    steps = 4 * depth - 4
    middle = steps // 2

    def receive(n, carry):
        panel = place(n)[2]
        for u in range(per):
            hand(panel, u).wait_recv()
            finish(1, panel, u, lambda t: landed[panel, u, t], False)
        return carry

    def nearby():
        for u in range(per):
            for p in range(2):
                parity = b if p == 0 else nb
                finish(p, w, u, cut(gram(p, lambda h, a: own[h, parity, u, a])), True)
        panel = at(z, y, 1 - c)
        for h in (b, nb):
            for t in range(per):
                arrive(h, t, panel)
            mate_arrive(h, 0)
        for u in range(per):
            finish(0, panel, u, cut(gram(0, lambda h, a: cols[h, panel, u, a])), False)
            finish(1, panel, u, cut(gram(1, lambda h, a: mate[h, 0, u, a])), False)

    def compute(n, carry):
        k, i, panel = place(n)
        ahead = k + 1 + inner

        @pl.when(jnp.logical_and(i == 2, k == 1))
        def _():
            nearby()

        @pl.when(jnp.logical_and(i == 2, jnp.logical_and(ahead > 1, ahead < depth)))
        def _():
            forward_z(ahead)

        @pl.when(jnp.logical_and(i == 2, k == 1))
        def _():
            relay_near(b)

        @pl.when(jnp.logical_and(i == 2, jnp.logical_and(k == 2, inner == 1)))
        def _():
            relay_far(b)

        @pl.when(jnp.logical_and(i == 2, k == last))
        def _():
            lax.fori_loop(0, middle, receive, 0)

        for u in range(per):
            @pl.when(i != 0)
            def _():
                for h in (b, nb):
                    arrive(h, u, panel)

            @pl.when(i == 2)
            def _():
                for h in (b, nb):
                    start(y_push(h, u, k))

            total = cut(gram(1, lambda h, a: cols[h, panel, u, a]))
            for t in range(per):
                stage[panel, u, t] = total(t)
            hand(panel, u).start()

        @pl.when(n == 0)
        def _():
            start(beside_push(nb))

        for u in range(per):
            finish(0, panel, u, cut(gram(0, lambda h, a: cols[h, panel, u, a])), False)

        @pl.when(jnp.logical_and(i == 3, k == 1))
        def _():
            relay_near(nb)

        @pl.when(jnp.logical_and(i == 3, jnp.logical_and(k == 2, inner == 1)))
        def _():
            relay_far(nb)

        return carry

    lax.fori_loop(0, steps, compute, 0)

    @pl.when(inner == 0)
    def _():
        for h in (b, nb):
            relay_far(h)

    def distant(n, carry):
        cc = jnp.where(n == 0, c, 1 - c)
        slot = jnp.where(n == 0, 1 + far, 3)
        panel = at(far_z, y, cc)

        @pl.when(n == 1)
        def _():
            for h in (b, nb):
                for t in range(per):
                    arrive(h, t, panel)
                mate_arrive(h, 3)

        for u in range(per):
            finish(0, panel, u, cut(gram(0, lambda h, a: cols[h, panel, u, a])), False)
            finish(1, panel, u, cut(gram(1, lambda h, a: mate[h, slot, u, a])), False)
        return carry

    lax.fori_loop(0, 2, distant, 0)
    lax.fori_loop(middle, steps, receive, 0)

    for i in range(2):
        for t in range(per):
            swap(b, i, t).wait_send()
    for h in (b, nb):
        for t in range(per):
            drain(own_pushes(h, t))
        drain(beside_push(h))
        drain(end_push(h))
        drain(relay_push(h, 1 - far, 2))
        drain(relay_push(h, far, 3))
        drain(far_push(h))

    def drain_group(k, carry):
        for h in (b, nb):
            for t in range(per):
                drain(y_push(h, t, k))

                @pl.when(k > 0)
                def _():
                    drain(z_pushes(h, t, k))
        return carry

    lax.fori_loop(0, depth, drain_group, 0)

    def drain_panel(n, carry):
        for u in range(per):
            hand(place(n)[2], u).wait_send()
        return carry

    lax.fori_loop(0, steps, drain_panel, 0)


def ring(resid, samples, precision, active):
    panels = lax.axis_size("wide")
    row_tiles, _, per_class, tile, _ = precision.shape
    per = row_tiles // 2
    half = resid.shape[1]
    depth = panels // 4
    scale = 0.5 / (2 * half)
    any_spec = pl.BlockSpec(memory_space=pl.ANY)
    bf16, f32 = resid.dtype, jnp.float32
    dma = pltpu.SemaphoreType.DMA
    updated = pl.pallas_call(
        functools.partial(kernel, depth, scale),
        out_shape=pltpu.VMEM((per, 2, per_class, tile, tile), f32),
        in_specs=[any_spec, any_spec, any_spec, pl.BlockSpec(memory_space=pltpu.SMEM)],
        out_specs=pl.BlockSpec(memory_space=pltpu.VMEM),
        scratch_shapes=[
            pltpu.VMEM((2, 2, per, 2, tile, half), bf16),
            pltpu.VMEM((2, panels, per, 2, tile, half), bf16),
            pltpu.VMEM((2, 4, per, 2, tile, half), bf16),
            pltpu.VMEM((panels, per, per, tile, tile), f32),
            pltpu.VMEM((panels, per, per, tile, tile), f32),
            dma((2, panels, per)),
            dma((2, per)),
            dma((panels, per)),
            dma((2, 4)),
            dma((2, per, depth, 5)),
            dma((2, per)),
            dma((panels, per)),
            dma((2, 5)),
            dma((5,)),
        ],
        compiler_params=pltpu.CompilerParams(
            collective_id=0, has_side_effects=True, vmem_limit_bytes=52 * 1024 * 1024
        ),
    )(
        resid.reshape(per, 2, tile, half),
        samples.reshape(per, 2, tile, half),
        precision.reshape(per, 2, per_class, tile, tile),
        active[:, 0],
    )
    return updated.reshape(precision.shape)


def body(resid, samples, precision, active):
    panels = lax.axis_size("wide")
    row_tiles, _, per_class, tile, _ = precision.shape
    words = 8 * per_class * row_tiles * tile * tile + 4 * panels * row_tiles * tile * resid.shape[1]
    if lax.axis_size("blk") == 2 and panels // 4 == 4 and row_tiles % 2 == 0 and words < 52 * 1024 * 1024:
        return ring(resid, samples, precision, active)
    return local(resid, samples, precision, active)


def solution(mesh):
    in_specs = (
        P("wide", "blk"),
        P("wide", "blk"),
        P("wide", "blk", None, None, None),
        P("wide", "blk", None),
    )
    out_specs = P("wide", "blk", None, None, None)
    return jax.shard_map(body, mesh=mesh, in_specs=in_specs, out_specs=out_specs, check_vma=False)
```

```python
import functools

import jax
import jax.numpy as jnp
from jax import lax
from jax.experimental import pallas as pl
from jax.experimental.pallas import tpu as pltpu
from jax.sharding import PartitionSpec as P

STEP = 1.0
LASSO = 0.1
RIDGE = 0.5


def local(resid, samples, precision, active):
    groups = lax.axis_size("blk")
    column_group = lax.axis_index("blk")
    panel_index = lax.axis_index("wide")
    row_tiles = precision.shape[0]
    per_class = precision.shape[2]
    tile_size = precision.shape[3]
    tiles = per_class * groups
    local_samples = resid.shape[1]
    total_samples = local_samples * groups
    own_rows = panel_index * row_tiles + jnp.arange(row_tiles, dtype=jnp.int32)
    first_column = (column_group - own_rows) % groups
    own_resid = resid.reshape(row_tiles, tile_size, local_samples)
    own_data = samples.reshape(row_tiles, tile_size, local_samples)
    all_resid, all_data = (
        lax.all_gather(resid, "wide", axis=0, tiled=True),
        lax.all_gather(samples, "wide", axis=0, tiled=True),
    )
    resid_tiles = all_resid.reshape(tiles, tile_size, local_samples)
    data_tiles = all_data.reshape(tiles, tile_size, local_samples)
    positions = jnp.arange(per_class * lax.axis_size("blk"), dtype=jnp.int32)
    classes = positions // per_class
    within = positions % per_class
    column_ids = (classes[:, None] - own_rows[None, :]) % groups + groups * within[:, None]
    forward = jnp.einsum(
        "kis,pkjs->pkij", own_resid, data_tiles[column_ids], preferred_element_type=jnp.float32
    )
    backward = jnp.einsum(
        "kis,pkjs->pkij", own_data, resid_tiles[column_ids], preferred_element_type=jnp.float32
    )
    summed = (
        lax.psum_scatter(0.5 * (forward + backward), "blk", scatter_dimension=0, tiled=True)
        / total_samples
    )
    precision_tiles = precision[:, 0]
    active_flags = active[:, 0].astype(jnp.float32)
    gradient_part = summed.transpose(1, 0, 2, 3)
    column_ids = first_column[:, None] + groups * jnp.arange(per_class, dtype=jnp.int32)[None, :]
    same_tile = column_ids == own_rows[:, None]
    identity = jnp.eye(tile_size, dtype=bool)
    on_diag = same_tile[:, :, None, None] & identity
    inverse = jnp.where(on_diag, 1.0 / jnp.where(on_diag, precision_tiles, 1.0), 0.0)
    stepped = precision_tiles - STEP * (gradient_part + RIDGE * precision_tiles - inverse)
    shrunk = jnp.sign(stepped) * jnp.maximum(jnp.abs(stepped) - STEP * LASSO, 0.0)
    updated = jnp.where(on_diag, stepped, shrunk) * active_flags[:, :, None, None]
    return updated[:, None]


MESH = pl.DeviceIdType.MESH


def pick(table, i):
    value = jnp.int32(table[0])
    for n in range(1, len(table)):
        value = jnp.where(i == n, jnp.int32(table[n]), value)
    return value


def kernel(
    depth, scale, resid, samples, weights, flags, held,
    own, cols, mate, stage, landed, recv, own_recv, res_recv, mate_recv, send, own_send, res_send,
    mate_send, fill,
):
    b = lax.axis_index("blk")
    w = lax.axis_index("wide")
    nb = 1 - b
    z, y, c = w // 4, (w // 2) % 2, w % 2
    per = own.shape[2]
    tile = own.shape[4]
    panels = cols.shape[1]
    up, down = (z + 1 < depth), (z > 0)
    last = depth - 1
    inner = jnp.where(up, 1, 0) * jnp.where(down, 1, 0)
    far = jnp.where(2 * z < depth, 1, 0)
    far_z = far * last

    def at(zz, yy, cc):
        return (zz * 2 + yy) * 2 + cc

    orders = [
        sorted((o for o in range(depth) if o != i), key=lambda o: (abs(o - i), o))
        for i in range(depth)
    ]

    def order(k):
        value = z
        for n in range(1, depth):
            value = jnp.where(k == n, pick([orders[i][n - 1] for i in range(depth)], z), value)
        return value

    loads = []
    for a, src in enumerate((resid, samples)):
        for p in range(2):
            loads.append(
                pltpu.make_async_copy(src.at[:, p], own.at[b, p, :, a], fill.at[2 * a + p])
            )
    for load in loads:
        load.start()
    load_weights = pltpu.make_async_copy(weights, held, fill.at[4])

    barrier = pltpu.get_barrier_semaphore()

    def greet(**device):
        pl.semaphore_signal(barrier, inc=1, device_id=device, device_id_type=MESH)

    greet(blk=nb)
    greet(wide=at(z, 1 - y, c))
    greet(wide=at(z, y, 1 - c))

    @pl.when(up)
    def _():
        greet(wide=at(z + 1, y, c))

    @pl.when(down)
    def _():
        greet(wide=at(z - 1, y, c))

    pl.semaphore_wait(barrier, 3 + jnp.where(up, 1, 0) + jnp.where(down, 1, 0))

    def push(h, t, src, panel, k, lane, target):
        return pltpu.make_async_remote_copy(
            src_ref=src, dst_ref=cols.at[h, panel, t], send_sem=send.at[h, t, k, lane],
            recv_sem=recv.at[h, panel, t], device_id={"wide": target}, device_id_type=MESH,
        )

    def arrive(h, t, panel):
        push(h, t, cols.at[h, panel, t], panel, 0, 0, at(z, 1 - y, c)).wait_recv()

    def own_pushes(h, t):
        src = own.at[h, b, t]
        return (
            (up, push(h, t, src, w, 0, 0, at(z + 1, y, c))),
            (down, push(h, t, src, w, 0, 1, at(z - 1, y, c))),
            (None, push(h, t, src, w, 0, 2, at(z, 1 - y, c))),
            (None, push(h, t, src, w, 0, 3, at(z, y, 1 - c))),
        )

    def z_pushes(h, t, k):
        zk = order(k)
        panel = at(zk, y, c)
        src = cols.at[h, panel, t]
        onward = jnp.where(zk < z, z + 1, z - 1)
        exists = jnp.logical_and(onward >= 0, onward < depth)
        return (
            (exists, push(h, t, src, panel, k, 0, at(onward, y, c))),
            (None, push(h, t, src, panel, k, 2, at(z, 1 - y, c))),
            (None, push(h, t, src, panel, k, 3, at(z, y, 1 - c))),
        )

    def y_push(h, t, k):
        panel = at(order(k), 1 - y, c)
        return ((None, push(h, t, cols.at[h, panel, t], panel, k, 4, at(z, y, 1 - c))),)

    def mate_push(h, src, slot, lane, target):
        return pltpu.make_async_remote_copy(
            src_ref=src, dst_ref=mate.at[h, slot], send_sem=mate_send.at[h, lane],
            recv_sem=mate_recv.at[h, slot], device_id={"wide": target}, device_id_type=MESH,
        )

    def beside_push(h):
        return ((None, mate_push(h, own.at[h, nb], 0, 0, at(z, y, 1 - c))),)

    def end_push(h):
        slot = jnp.where(z == 0, 1, 2)
        inward = jnp.where(z == 0, z + 1, z - 1)
        return ((inner == 0, mate_push(h, own.at[h, nb], slot, 1, at(inward, y, c))),)

    def relay_push(h, end, lane):
        onward = jnp.where(end == 0, z + 1, z - 1)
        return ((inner == 1, mate_push(h, mate.at[h, 1 + end], 1 + end, lane, at(onward, y, c))),)

    def far_push(h):
        return ((None, mate_push(h, mate.at[h, 1 + far], 3, 4, at(z, y, 1 - c))),)

    def mate_arrive(h, slot):
        mate_push(h, mate.at[h, slot], slot, 0, at(z, y, 1 - c)).wait_recv()

    def start(pushes):
        for when, copy in pushes:
            if when is None:
                copy.start()
            else:
                pl.when(when)(copy.start)

    def drain(pushes):
        for when, copy in pushes:
            if when is None:
                copy.wait_send()
            else:
                pl.when(when)(copy.wait_send)

    def forward_z(k):
        for t in range(per):
            for h in (b, nb):
                arrive(h, t, at(order(k), y, c))
                start(z_pushes(h, t, k))

    def relay_near(h):
        @pl.when(inner == 1)
        def _():
            mate_arrive(h, 2 - far)
            start(relay_push(h, 1 - far, 2))

    def relay_far(h):
        mate_arrive(h, 1 + far)
        start(relay_push(h, far, 3))
        start(far_push(h))

    def swap(h, i, t):
        p = (nb, b)[i] if h is b else (b, nb)[i]
        return pltpu.make_async_remote_copy(
            src_ref=own.at[h, p, t], dst_ref=own.at[h, p, t], send_sem=own_send.at[i, t],
            recv_sem=own_recv.at[i, t], device_id={"blk": nb}, device_id_type=MESH,
        )

    def hand(panel, u):
        return pltpu.make_async_remote_copy(
            src_ref=stage.at[panel, u], dst_ref=landed.at[panel, u],
            send_sem=res_send.at[panel, u], recv_sem=res_recv.at[panel, u],
            device_id={"blk": nb}, device_id_type=MESH,
        )

    def gram(p, side):
        total = None
        for h in range(2):
            for a in range(2):
                left = own[h, p, :, a].reshape(per * tile, -1)
                right = side(h, 1 - a).reshape(-1, own.shape[5])
                part = lax.dot_general(
                    left, right, (((1,), (1,)), ((), ())), preferred_element_type=jnp.float32
                )
                total = part if total is None else total + part
        return total * scale

    def finish(p, panel, u, part, diagonal):
        for t in range(per):
            slot = panel * per + u
            weight = held[t, p, slot]
            half = part(t) + RIDGE * weight
            if diagonal and t == u:
                rows = lax.broadcasted_iota(jnp.int32, (tile, tile), 0)
                columns = lax.broadcasted_iota(jnp.int32, (tile, tile), 1)
                on_diag = rows == columns + b * (2 * tile)
                inverse = jnp.where(on_diag, 1.0 / jnp.where(on_diag, weight, 1.0), 0.0)
                stepped = weight - STEP * (half - inverse)
            else:
                stepped = weight - STEP * half
            bound = STEP * LASSO
            updated = stepped - jnp.clip(stepped, -bound, bound)
            if diagonal and t == u:
                updated = jnp.where(on_diag, stepped, updated)
            flag = flags[2 * t + p, slot].astype(jnp.float32)
            held[t, p, slot] = updated * flag

    def cut(total, u=0):
        return lambda t: total[t * tile:(t + 1) * tile, u * tile:(u + 1) * tile]

    def finish_all(p, panel, total, diagonal):
        for u in range(per):
            finish(p, panel, u, cut(total, u), diagonal)

    for load in loads:
        load.wait()
    for i in range(2):
        for t in range(per):
            swap(b, i, t).start()
    for t in range(per):
        start(own_pushes(b, t))
    load_weights.start()
    for t in range(per):
        swap(nb, 0, t).wait_recv()
        start(own_pushes(nb, t))
    start(end_push(b))
    start(beside_push(b))
    for h in (b, nb):
        for t in range(per):
            arrive(h, t, at(order(1), y, c))
            start(z_pushes(h, t, 1))

            @pl.when(inner == 1)
            def _():
                arrive(h, t, at(order(2), y, c))
                start(z_pushes(h, t, 2))
    for t in range(per):
        swap(nb, 1, t).wait_recv()
    start(end_push(nb))
    load_weights.wait()

    def place(n):
        s = n + 2 + jnp.where(n < 4 * depth - 6, 0, 2)
        k, i = s // 4, s % 4
        yy = jnp.where(i < 2, y, 1 - y)
        cc = jnp.where(i % 2 == 0, c, 1 - c)
        return k, i, at(order(k), yy, cc)

    steps = 4 * depth - 4
    middle = steps - 4

    def receive(n, carry):
        panel = place(n)[2]
        for u in range(per):
            hand(panel, u).wait_recv()
            finish(1, panel, u, lambda t: landed[panel, u, t], False)
        return carry

    def keep(panel):
        finish_all(0, panel, gram(0, lambda h, a: cols[h, panel, :, a]), False)

    def nearby():
        for p in range(2):
            parity = b if p == 0 else nb
            finish_all(p, w, gram(p, lambda h, a: own[h, parity, :, a]), True)
        panel = at(z, y, 1 - c)
        for h in (b, nb):
            for t in range(per):
                arrive(h, t, panel)
            mate_arrive(h, 0)
        keep(panel)
        finish_all(1, panel, gram(1, lambda h, a: mate[h, 0, :, a]), False)

    def compute(n, carry):
        k, i, panel = place(n)
        ahead = k + 1 + inner

        @pl.when(jnp.logical_and(i == 2, k == 1))
        def _():
            nearby()

        @pl.when(jnp.logical_and(i == 2, jnp.logical_and(k > 0, ahead < depth)))
        def _():
            forward_z(ahead)

        @pl.when(jnp.logical_and(i == 2, k == 1))
        def _():
            relay_near(b)

        @pl.when(jnp.logical_and(i == 2, jnp.logical_and(k == 2, inner == 1)))
        def _():
            relay_far(b)

        @pl.when(jnp.logical_and(i == 2, k == last))
        def _():
            lax.fori_loop(0, middle, receive, 0)

        for u in range(per):
            @pl.when(i != 0)
            def _():
                for h in (b, nb):
                    arrive(h, u, panel)

            @pl.when(i == 2)
            def _():
                for h in (b, nb):
                    start(y_push(h, u, k))

            total = cut(gram(1, lambda h, a: cols[h, panel, u, a]))
            for t in range(per):
                stage[panel, u, t] = total(t)
            hand(panel, u).start()

        @pl.when(n == 0)
        def _():
            start(beside_push(nb))

        @pl.when(k < last)
        def _():
            keep(panel)

        @pl.when(jnp.logical_and(i == 3, k == 1))
        def _():
            relay_near(nb)

        @pl.when(jnp.logical_and(i == 3, jnp.logical_and(k == 2, inner == 1)))
        def _():
            relay_far(nb)

        return carry

    lax.fori_loop(0, steps, compute, 0)

    def keep_late(n, carry):
        keep(place(n)[2])
        return carry

    lax.fori_loop(steps - 2, steps, keep_late, 0)

    @pl.when(inner == 0)
    def _():
        for h in (b, nb):
            relay_far(h)

    def distant(n, carry):
        cc = jnp.where(n == 0, c, 1 - c)
        slot = jnp.where(n == 0, 1 + far, 3)
        panel = at(far_z, y, cc)

        @pl.when(n == 1)
        def _():
            for h in (b, nb):
                for t in range(per):
                    arrive(h, t, panel)
                mate_arrive(h, 3)

        keep(panel)
        finish_all(1, panel, gram(1, lambda h, a: mate[h, slot, :, a]), False)
        return carry

    lax.fori_loop(0, 2, distant, 0)
    lax.fori_loop(middle, steps, receive, 0)

    for i in range(2):
        for t in range(per):
            swap(b, i, t).wait_send()
    for h in (b, nb):
        for t in range(per):
            drain(own_pushes(h, t))
        drain(beside_push(h))
        drain(end_push(h))
        drain(relay_push(h, 1 - far, 2))
        drain(relay_push(h, far, 3))
        drain(far_push(h))

    def drain_group(k, carry):
        for h in (b, nb):
            for t in range(per):
                drain(y_push(h, t, k))

                @pl.when(k > 0)
                def _():
                    drain(z_pushes(h, t, k))
        return carry

    lax.fori_loop(0, depth, drain_group, 0)

    def drain_panel(n, carry):
        for u in range(per):
            hand(place(n)[2], u).wait_send()
        return carry

    lax.fori_loop(0, steps, drain_panel, 0)


def ring(resid, samples, precision, active):
    panels = lax.axis_size("wide")
    row_tiles, _, per_class, tile, _ = precision.shape
    per = row_tiles // 2
    half = resid.shape[1]
    depth = panels // 4
    scale = 0.5 / (2 * half)
    any_spec = pl.BlockSpec(memory_space=pl.ANY)
    bf16, f32 = resid.dtype, jnp.float32
    dma = pltpu.SemaphoreType.DMA
    updated = pl.pallas_call(
        functools.partial(kernel, depth, scale),
        out_shape=pltpu.VMEM((per, 2, per_class, tile, tile), f32),
        in_specs=[any_spec, any_spec, any_spec, pl.BlockSpec(memory_space=pltpu.SMEM)],
        out_specs=pl.BlockSpec(memory_space=pltpu.VMEM),
        scratch_shapes=[
            pltpu.VMEM((2, 2, per, 2, tile, half), bf16),
            pltpu.VMEM((2, panels, per, 2, tile, half), bf16),
            pltpu.VMEM((2, 4, per, 2, tile, half), bf16),
            pltpu.VMEM((panels, per, per, tile, tile), f32),
            pltpu.VMEM((panels, per, per, tile, tile), f32),
            dma((2, panels, per)),
            dma((2, per)),
            dma((panels, per)),
            dma((2, 4)),
            dma((2, per, depth, 5)),
            dma((2, per)),
            dma((panels, per)),
            dma((2, 5)),
            dma((5,)),
        ],
        compiler_params=pltpu.CompilerParams(
            collective_id=0, has_side_effects=True, vmem_limit_bytes=52 * 1024 * 1024
        ),
    )(
        resid.reshape(per, 2, tile, half),
        samples.reshape(per, 2, tile, half),
        precision.reshape(per, 2, per_class, tile, tile),
        active[:, 0],
    )
    return updated.reshape(precision.shape)


def body(resid, samples, precision, active):
    panels = lax.axis_size("wide")
    row_tiles, _, per_class, tile, _ = precision.shape
    words = 8 * per_class * row_tiles * tile * tile + 4 * panels * row_tiles * tile * resid.shape[1]
    if lax.axis_size("blk") == 2 and panels // 4 == 4 and row_tiles % 2 == 0 and words < 52 * 1024 * 1024:
        return ring(resid, samples, precision, active)
    return local(resid, samples, precision, active)


def solution(mesh):
    in_specs = (
        P("wide", "blk"),
        P("wide", "blk"),
        P("wide", "blk", None, None, None),
        P("wide", "blk", None),
    )
    out_specs = P("wide", "blk", None, None, None)
    return jax.shard_map(body, mesh=mesh, in_specs=in_specs, out_specs=out_specs, check_vma=False)
```

```python
import functools

import jax
import jax.numpy as jnp
from jax import lax
from jax.experimental import pallas as pl
from jax.experimental.pallas import tpu as pltpu
from jax.sharding import PartitionSpec as P

STEP = 1.0
LASSO = 0.1
RIDGE = 0.5


def local(resid, samples, precision, active):
    groups = lax.axis_size("blk")
    column_group = lax.axis_index("blk")
    panel_index = lax.axis_index("wide")
    row_tiles = precision.shape[0]
    per_class = precision.shape[2]
    tile_size = precision.shape[3]
    tiles = per_class * groups
    local_samples = resid.shape[1]
    total_samples = local_samples * groups
    own_rows = panel_index * row_tiles + jnp.arange(row_tiles, dtype=jnp.int32)
    first_column = (column_group - own_rows) % groups
    own_resid = resid.reshape(row_tiles, tile_size, local_samples)
    own_data = samples.reshape(row_tiles, tile_size, local_samples)
    all_resid, all_data = (
        lax.all_gather(resid, "wide", axis=0, tiled=True),
        lax.all_gather(samples, "wide", axis=0, tiled=True),
    )
    resid_tiles = all_resid.reshape(tiles, tile_size, local_samples)
    data_tiles = all_data.reshape(tiles, tile_size, local_samples)
    positions = jnp.arange(per_class * lax.axis_size("blk"), dtype=jnp.int32)
    classes = positions // per_class
    within = positions % per_class
    column_ids = (classes[:, None] - own_rows[None, :]) % groups + groups * within[:, None]
    forward = jnp.einsum(
        "kis,pkjs->pkij", own_resid, data_tiles[column_ids], preferred_element_type=jnp.float32
    )
    backward = jnp.einsum(
        "kis,pkjs->pkij", own_data, resid_tiles[column_ids], preferred_element_type=jnp.float32
    )
    summed = (
        lax.psum_scatter(0.5 * (forward + backward), "blk", scatter_dimension=0, tiled=True)
        / total_samples
    )
    precision_tiles = precision[:, 0]
    active_flags = active[:, 0].astype(jnp.float32)
    gradient_part = summed.transpose(1, 0, 2, 3)
    column_ids = first_column[:, None] + groups * jnp.arange(per_class, dtype=jnp.int32)[None, :]
    same_tile = column_ids == own_rows[:, None]
    identity = jnp.eye(tile_size, dtype=bool)
    on_diag = same_tile[:, :, None, None] & identity
    inverse = jnp.where(on_diag, 1.0 / jnp.where(on_diag, precision_tiles, 1.0), 0.0)
    stepped = precision_tiles - STEP * (gradient_part + RIDGE * precision_tiles - inverse)
    shrunk = jnp.sign(stepped) * jnp.maximum(jnp.abs(stepped) - STEP * LASSO, 0.0)
    updated = jnp.where(on_diag, stepped, shrunk) * active_flags[:, :, None, None]
    return updated[:, None]


MESH = pl.DeviceIdType.MESH


def pick(table, i):
    value = jnp.int32(table[0])
    for n in range(1, len(table)):
        value = jnp.where(i == n, jnp.int32(table[n]), value)
    return value


def kernel(
    depth, scale, resid, samples, weights, flags, held,
    own, cols, mate, stage, landed, recv, own_recv, res_recv, mate_recv, send, own_send, res_send,
    mate_send, fill,
):
    b = lax.axis_index("blk")
    w = lax.axis_index("wide")
    nb = 1 - b
    z, y, c = w // 4, (w // 2) % 2, w % 2
    per = own.shape[2]
    tile = own.shape[4]
    panels = cols.shape[1]
    up, down = (z + 1 < depth), (z > 0)
    last = depth - 1
    inner = jnp.where(up, 1, 0) * jnp.where(down, 1, 0)
    far = jnp.where(2 * z < depth, 1, 0)
    far_z = far * last

    def at(zz, yy, cc):
        return (zz * 2 + yy) * 2 + cc

    orders = [
        sorted((o for o in range(depth) if o != i), key=lambda o: (abs(o - i), o))
        for i in range(depth)
    ]

    def order(k):
        value = z
        for n in range(1, depth):
            value = jnp.where(k == n, pick([orders[i][n - 1] for i in range(depth)], z), value)
        return value

    loads = []
    for a, src in enumerate((resid, samples)):
        for p in range(2):
            loads.append(
                pltpu.make_async_copy(src.at[:, p], own.at[b, p, :, a], fill.at[2 * a + p])
            )
    for load in loads:
        load.start()
    load_weights = pltpu.make_async_copy(weights, held, fill.at[4])

    barrier = pltpu.get_barrier_semaphore()

    def greet(**device):
        pl.semaphore_signal(barrier, inc=1, device_id=device, device_id_type=MESH)

    greet(blk=nb)
    greet(wide=at(z, 1 - y, c))
    greet(wide=at(z, y, 1 - c))

    @pl.when(up)
    def _():
        greet(wide=at(z + 1, y, c))

    @pl.when(down)
    def _():
        greet(wide=at(z - 1, y, c))

    pl.semaphore_wait(barrier, 3 + jnp.where(up, 1, 0) + jnp.where(down, 1, 0))

    def push(h, t, src, panel, k, lane, target):
        return pltpu.make_async_remote_copy(
            src_ref=src, dst_ref=cols.at[h, panel, t], send_sem=send.at[h, t, k, lane],
            recv_sem=recv.at[h, panel, t], device_id={"wide": target}, device_id_type=MESH,
        )

    def arrive(h, t, panel):
        push(h, t, cols.at[h, panel, t], panel, 0, 0, at(z, 1 - y, c)).wait_recv()

    def own_pushes(h, t):
        src = own.at[h, b, t]
        return (
            (up, push(h, t, src, w, 0, 0, at(z + 1, y, c))),
            (down, push(h, t, src, w, 0, 1, at(z - 1, y, c))),
            (None, push(h, t, src, w, 0, 2, at(z, 1 - y, c))),
            (None, push(h, t, src, w, 0, 3, at(z, y, 1 - c))),
        )

    def z_pushes(h, t, k):
        zk = order(k)
        panel = at(zk, y, c)
        src = cols.at[h, panel, t]
        onward = jnp.where(zk < z, z + 1, z - 1)
        exists = jnp.logical_and(onward >= 0, onward < depth)
        return (
            (exists, push(h, t, src, panel, k, 0, at(onward, y, c))),
            (None, push(h, t, src, panel, k, 2, at(z, 1 - y, c))),
            (None, push(h, t, src, panel, k, 3, at(z, y, 1 - c))),
        )

    def y_push(h, t, k):
        panel = at(order(k), 1 - y, c)
        return ((None, push(h, t, cols.at[h, panel, t], panel, k, 4, at(z, y, 1 - c))),)

    def mate_push(h, src, slot, lane, target):
        return pltpu.make_async_remote_copy(
            src_ref=src, dst_ref=mate.at[h, slot], send_sem=mate_send.at[h, lane],
            recv_sem=mate_recv.at[h, slot], device_id={"wide": target}, device_id_type=MESH,
        )

    def beside_push(h):
        return ((None, mate_push(h, own.at[h, nb], 0, 0, at(z, y, 1 - c))),)

    def end_push(h):
        slot = jnp.where(z == 0, 1, 2)
        inward = jnp.where(z == 0, z + 1, z - 1)
        return ((inner == 0, mate_push(h, own.at[h, nb], slot, 1, at(inward, y, c))),)

    def relay_push(h, end, lane):
        onward = jnp.where(end == 0, z + 1, z - 1)
        return ((inner == 1, mate_push(h, mate.at[h, 1 + end], 1 + end, lane, at(onward, y, c))),)

    def far_push(h):
        return ((None, mate_push(h, mate.at[h, 1 + far], 3, 4, at(z, y, 1 - c))),)

    def mate_arrive(h, slot):
        mate_push(h, mate.at[h, slot], slot, 0, at(z, y, 1 - c)).wait_recv()

    def start(pushes):
        for when, copy in pushes:
            if when is None:
                copy.start()
            else:
                pl.when(when)(copy.start)

    def drain(pushes):
        for when, copy in pushes:
            if when is None:
                copy.wait_send()
            else:
                pl.when(when)(copy.wait_send)

    def forward_z(k):
        for t in range(per):
            for h in (b, nb):
                arrive(h, t, at(order(k), y, c))
                start(z_pushes(h, t, k))

    def relay_near(h):
        @pl.when(inner == 1)
        def _():
            mate_arrive(h, 2 - far)
            start(relay_push(h, 1 - far, 2))

    def relay_far(h):
        mate_arrive(h, 1 + far)
        start(relay_push(h, far, 3))
        start(far_push(h))

    def swap(h, i, t):
        p = (nb, b)[i] if h is b else (b, nb)[i]
        return pltpu.make_async_remote_copy(
            src_ref=own.at[h, p, t], dst_ref=own.at[h, p, t], send_sem=own_send.at[i, t],
            recv_sem=own_recv.at[i, t], device_id={"blk": nb}, device_id_type=MESH,
        )

    def hand(panel, u):
        return pltpu.make_async_remote_copy(
            src_ref=stage.at[panel, u], dst_ref=landed.at[panel, u],
            send_sem=res_send.at[panel, u], recv_sem=res_recv.at[panel, u],
            device_id={"blk": nb}, device_id_type=MESH,
        )

    def gram(p, side):
        total = None
        for h in range(2):
            for a in range(2):
                left = own[h, p, :, a].reshape(per * tile, -1)
                right = side(h, 1 - a).reshape(-1, own.shape[5])
                part = lax.dot_general(
                    left, right, (((1,), (1,)), ((), ())), preferred_element_type=jnp.float32
                )
                total = part if total is None else total + part
        return total * scale

    def finish(p, panel, u, part, diagonal):
        for t in range(per):
            slot = panel * per + u
            weight = held[t, p, slot]
            half = part(t) + RIDGE * weight
            if diagonal and t == u:
                rows = lax.broadcasted_iota(jnp.int32, (tile, tile), 0)
                columns = lax.broadcasted_iota(jnp.int32, (tile, tile), 1)
                on_diag = rows == columns + b * (2 * tile)
                inverse = jnp.where(on_diag, 1.0 / jnp.where(on_diag, weight, 1.0), 0.0)
                stepped = weight - STEP * (half - inverse)
            else:
                stepped = weight - STEP * half
            bound = STEP * LASSO
            updated = stepped - jnp.clip(stepped, -bound, bound)
            if diagonal and t == u:
                updated = jnp.where(on_diag, stepped, updated)
            flag = flags[2 * t + p, slot].astype(jnp.float32)
            held[t, p, slot] = updated * flag

    def cut(total, u=0):
        return lambda t: total[t * tile:(t + 1) * tile, u * tile:(u + 1) * tile]

    def finish_all(p, panel, total, diagonal):
        for u in range(per):
            finish(p, panel, u, cut(total, u), diagonal)

    for load in loads:
        load.wait()
    for i in range(2):
        for t in range(per):
            swap(b, i, t).start()
    for t in range(per):
        start(own_pushes(b, t))
    load_weights.start()
    for t in range(per):
        swap(nb, 0, t).wait_recv()
        start(own_pushes(nb, t))
    start(end_push(b))
    start(beside_push(b))
    for h in (b, nb):
        for t in range(per):
            arrive(h, t, at(order(1), y, c))
            start(z_pushes(h, t, 1))

            @pl.when(inner == 1)
            def _():
                arrive(h, t, at(order(2), y, c))
                start(z_pushes(h, t, 2)[:1])
    for t in range(per):
        swap(nb, 1, t).wait_recv()
    start(end_push(nb))
    load_weights.wait()

    def place(n):
        s = n + 2 + jnp.where(n < 4 * depth - 6, 0, 2)
        k, i = s // 4, s % 4
        yy = jnp.where(i < 2, y, 1 - y)
        cc = jnp.where(i % 2 == 0, c, 1 - c)
        return k, i, at(order(k), yy, cc)

    steps = 4 * depth - 4
    middle = steps - 4

    def receive(n, carry):
        panel = place(n)[2]
        for u in range(per):
            hand(panel, u).wait_recv()
            finish(1, panel, u, lambda t: landed[panel, u, t], False)
        return carry

    def keep(panel):
        finish_all(0, panel, gram(0, lambda h, a: cols[h, panel, :, a]), False)

    def nearby():
        for p in range(2):
            parity = b if p == 0 else nb
            finish_all(p, w, gram(p, lambda h, a: own[h, parity, :, a]), True)
        panel = at(z, y, 1 - c)
        for h in (b, nb):
            for t in range(per):
                arrive(h, t, panel)
            mate_arrive(h, 0)
        keep(panel)
        finish_all(1, panel, gram(1, lambda h, a: mate[h, 0, :, a]), False)

    def compute(n, carry):
        k, i, panel = place(n)
        ahead = k + 1 + inner

        @pl.when(jnp.logical_and(i == 2, k == 1))
        def _():
            nearby()

        @pl.when(jnp.logical_and(n == 0, inner == 1))
        def _():
            for t in range(per):
                for h in (b, nb):
                    start(z_pushes(h, t, 2)[1:])

        @pl.when(jnp.logical_and(i == 2, jnp.logical_and(k > 0, ahead < depth)))
        def _():
            forward_z(ahead)

        @pl.when(jnp.logical_and(i == 2, k == 1))
        def _():
            relay_near(b)

        @pl.when(jnp.logical_and(i == 2, jnp.logical_and(k == 2, inner == 1)))
        def _():
            relay_far(b)

        @pl.when(jnp.logical_and(i == 2, k == last))
        def _():
            lax.fori_loop(0, middle, receive, 0)

        for u in range(per):
            @pl.when(i != 0)
            def _():
                for h in (b, nb):
                    arrive(h, u, panel)

            @pl.when(i == 2)
            def _():
                for h in (b, nb):
                    start(y_push(h, u, k))

            total = cut(gram(1, lambda h, a: cols[h, panel, u, a]))
            for t in range(per):
                stage[panel, u, t] = total(t)
            hand(panel, u).start()

        @pl.when(n == 0)
        def _():
            start(beside_push(nb))

        @pl.when(k < last)
        def _():
            keep(panel)

        @pl.when(jnp.logical_and(i == 3, k == 1))
        def _():
            relay_near(nb)

        @pl.when(jnp.logical_and(i == 3, jnp.logical_and(k == 2, inner == 1)))
        def _():
            relay_far(nb)

        return carry

    lax.fori_loop(0, steps, compute, 0)

    def keep_late(n, carry):
        keep(place(n)[2])
        return carry

    lax.fori_loop(steps - 2, steps, keep_late, 0)

    @pl.when(inner == 0)
    def _():
        for h in (b, nb):
            relay_far(h)

    def distant(n, carry):
        cc = jnp.where(n == 0, c, 1 - c)
        slot = jnp.where(n == 0, 1 + far, 3)
        panel = at(far_z, y, cc)

        @pl.when(n == 1)
        def _():
            for h in (b, nb):
                for t in range(per):
                    arrive(h, t, panel)
                mate_arrive(h, 3)

        keep(panel)
        finish_all(1, panel, gram(1, lambda h, a: mate[h, slot, :, a]), False)
        return carry

    lax.fori_loop(0, 2, distant, 0)
    lax.fori_loop(middle, steps, receive, 0)

    for i in range(2):
        for t in range(per):
            swap(b, i, t).wait_send()
    for h in (b, nb):
        for t in range(per):
            drain(own_pushes(h, t))
        drain(beside_push(h))
        drain(end_push(h))
        drain(relay_push(h, 1 - far, 2))
        drain(relay_push(h, far, 3))
        drain(far_push(h))

    def drain_group(k, carry):
        for h in (b, nb):
            for t in range(per):
                drain(y_push(h, t, k))

                @pl.when(k > 0)
                def _():
                    drain(z_pushes(h, t, k))
        return carry

    lax.fori_loop(0, depth, drain_group, 0)

    def drain_panel(n, carry):
        for u in range(per):
            hand(place(n)[2], u).wait_send()
        return carry

    lax.fori_loop(0, steps, drain_panel, 0)


def ring(resid, samples, precision, active):
    panels = lax.axis_size("wide")
    row_tiles, _, per_class, tile, _ = precision.shape
    per = row_tiles // 2
    half = resid.shape[1]
    depth = panels // 4
    scale = 0.5 / (2 * half)
    any_spec = pl.BlockSpec(memory_space=pl.ANY)
    bf16, f32 = resid.dtype, jnp.float32
    dma = pltpu.SemaphoreType.DMA
    updated = pl.pallas_call(
        functools.partial(kernel, depth, scale),
        out_shape=pltpu.VMEM((per, 2, per_class, tile, tile), f32),
        in_specs=[any_spec, any_spec, any_spec, pl.BlockSpec(memory_space=pltpu.SMEM)],
        out_specs=pl.BlockSpec(memory_space=pltpu.VMEM),
        scratch_shapes=[
            pltpu.VMEM((2, 2, per, 2, tile, half), bf16),
            pltpu.VMEM((2, panels, per, 2, tile, half), bf16),
            pltpu.VMEM((2, 4, per, 2, tile, half), bf16),
            pltpu.VMEM((panels, per, per, tile, tile), f32),
            pltpu.VMEM((panels, per, per, tile, tile), f32),
            dma((2, panels, per)),
            dma((2, per)),
            dma((panels, per)),
            dma((2, 4)),
            dma((2, per, depth, 5)),
            dma((2, per)),
            dma((panels, per)),
            dma((2, 5)),
            dma((5,)),
        ],
        compiler_params=pltpu.CompilerParams(
            collective_id=0, has_side_effects=True, vmem_limit_bytes=52 * 1024 * 1024
        ),
    )(
        resid.reshape(per, 2, tile, half),
        samples.reshape(per, 2, tile, half),
        precision.reshape(per, 2, per_class, tile, tile),
        active[:, 0],
    )
    return updated.reshape(precision.shape)


def body(resid, samples, precision, active):
    panels = lax.axis_size("wide")
    row_tiles, _, per_class, tile, _ = precision.shape
    words = 8 * per_class * row_tiles * tile * tile + 4 * panels * row_tiles * tile * resid.shape[1]
    if lax.axis_size("blk") == 2 and panels // 4 == 4 and row_tiles % 2 == 0 and words < 52 * 1024 * 1024:
        return ring(resid, samples, precision, active)
    return local(resid, samples, precision, active)


def solution(mesh):
    in_specs = (
        P("wide", "blk"),
        P("wide", "blk"),
        P("wide", "blk", None, None, None),
        P("wide", "blk", None),
    )
    out_specs = P("wide", "blk", None, None, None)
    return jax.shard_map(body, mesh=mesh, in_specs=in_specs, out_specs=out_specs, check_vma=False)
```

```python
import functools

import jax
import jax.numpy as jnp
from jax import lax
from jax.experimental import pallas as pl
from jax.experimental.pallas import tpu as pltpu
from jax.sharding import PartitionSpec as P

STEP = 1.0
LASSO = 0.1
RIDGE = 0.5


def local(resid, samples, precision, active):
    groups = lax.axis_size("blk")
    column_group = lax.axis_index("blk")
    panel_index = lax.axis_index("wide")
    row_tiles = precision.shape[0]
    per_class = precision.shape[2]
    tile_size = precision.shape[3]
    tiles = per_class * groups
    local_samples = resid.shape[1]
    total_samples = local_samples * groups
    own_rows = panel_index * row_tiles + jnp.arange(row_tiles, dtype=jnp.int32)
    first_column = (column_group - own_rows) % groups
    own_resid = resid.reshape(row_tiles, tile_size, local_samples)
    own_data = samples.reshape(row_tiles, tile_size, local_samples)
    all_resid, all_data = (
        lax.all_gather(resid, "wide", axis=0, tiled=True),
        lax.all_gather(samples, "wide", axis=0, tiled=True),
    )
    resid_tiles = all_resid.reshape(tiles, tile_size, local_samples)
    data_tiles = all_data.reshape(tiles, tile_size, local_samples)
    positions = jnp.arange(per_class * lax.axis_size("blk"), dtype=jnp.int32)
    classes = positions // per_class
    within = positions % per_class
    column_ids = (classes[:, None] - own_rows[None, :]) % groups + groups * within[:, None]
    forward = jnp.einsum(
        "kis,pkjs->pkij", own_resid, data_tiles[column_ids], preferred_element_type=jnp.float32
    )
    backward = jnp.einsum(
        "kis,pkjs->pkij", own_data, resid_tiles[column_ids], preferred_element_type=jnp.float32
    )
    summed = (
        lax.psum_scatter(0.5 * (forward + backward), "blk", scatter_dimension=0, tiled=True)
        / total_samples
    )
    precision_tiles = precision[:, 0]
    active_flags = active[:, 0].astype(jnp.float32)
    gradient_part = summed.transpose(1, 0, 2, 3)
    column_ids = first_column[:, None] + groups * jnp.arange(per_class, dtype=jnp.int32)[None, :]
    same_tile = column_ids == own_rows[:, None]
    identity = jnp.eye(tile_size, dtype=bool)
    on_diag = same_tile[:, :, None, None] & identity
    inverse = jnp.where(on_diag, 1.0 / jnp.where(on_diag, precision_tiles, 1.0), 0.0)
    stepped = precision_tiles - STEP * (gradient_part + RIDGE * precision_tiles - inverse)
    shrunk = jnp.sign(stepped) * jnp.maximum(jnp.abs(stepped) - STEP * LASSO, 0.0)
    updated = jnp.where(on_diag, stepped, shrunk) * active_flags[:, :, None, None]
    return updated[:, None]


MESH = pl.DeviceIdType.MESH


def pick(table, i):
    value = jnp.int32(table[0])
    for n in range(1, len(table)):
        value = jnp.where(i == n, jnp.int32(table[n]), value)
    return value


def kernel(
    depth, scale, resid, samples, weights, flags, held,
    own, cols, mate, stage, landed, recv, own_recv, res_recv, mate_recv, send, own_send, res_send,
    mate_send, fill,
):
    b = lax.axis_index("blk")
    w = lax.axis_index("wide")
    nb = 1 - b
    z, y, c = w // 4, (w // 2) % 2, w % 2
    per = own.shape[2]
    tile = own.shape[4]
    panels = cols.shape[1]
    up, down = (z + 1 < depth), (z > 0)
    last = depth - 1
    inner = jnp.where(up, 1, 0) * jnp.where(down, 1, 0)
    far = jnp.where(2 * z < depth, 1, 0)
    far_z = far * last

    def at(zz, yy, cc):
        return (zz * 2 + yy) * 2 + cc

    orders = [
        sorted((o for o in range(depth) if o != i), key=lambda o: (abs(o - i), o))
        for i in range(depth)
    ]

    def order(k):
        value = z
        for n in range(1, depth):
            value = jnp.where(k == n, pick([orders[i][n - 1] for i in range(depth)], z), value)
        return value

    loads = []
    for a, src in enumerate((resid, samples)):
        for p in range(2):
            loads.append(
                pltpu.make_async_copy(src.at[:, p], own.at[b, p, :, a], fill.at[2 * a + p])
            )
    for load in loads:
        load.start()
    load_weights = pltpu.make_async_copy(weights, held, fill.at[4])

    barrier = pltpu.get_barrier_semaphore()

    def greet(**device):
        pl.semaphore_signal(barrier, inc=1, device_id=device, device_id_type=MESH)

    greet(blk=nb)
    greet(wide=at(z, 1 - y, c))
    greet(wide=at(z, y, 1 - c))

    @pl.when(up)
    def _():
        greet(wide=at(z + 1, y, c))

    @pl.when(down)
    def _():
        greet(wide=at(z - 1, y, c))

    pl.semaphore_wait(barrier, 3 + jnp.where(up, 1, 0) + jnp.where(down, 1, 0))

    def push(h, t, src, panel, k, lane, target):
        return pltpu.make_async_remote_copy(
            src_ref=src, dst_ref=cols.at[h, panel, t], send_sem=send.at[h, t, k, lane],
            recv_sem=recv.at[h, panel, t], device_id={"wide": target}, device_id_type=MESH,
        )

    def arrive(h, t, panel):
        push(h, t, cols.at[h, panel, t], panel, 0, 0, at(z, 1 - y, c)).wait_recv()

    def own_pushes(h, t):
        src = own.at[h, b, t]
        return (
            (up, push(h, t, src, w, 0, 0, at(z + 1, y, c))),
            (down, push(h, t, src, w, 0, 1, at(z - 1, y, c))),
            (None, push(h, t, src, w, 0, 2, at(z, 1 - y, c))),
            (None, push(h, t, src, w, 0, 3, at(z, y, 1 - c))),
        )

    def z_pushes(h, t, k):
        zk = order(k)
        panel = at(zk, y, c)
        src = cols.at[h, panel, t]
        onward = jnp.where(zk < z, z + 1, z - 1)
        exists = jnp.logical_and(onward >= 0, onward < depth)
        return (
            (exists, push(h, t, src, panel, k, 0, at(onward, y, c))),
            (None, push(h, t, src, panel, k, 2, at(z, 1 - y, c))),
            (None, push(h, t, src, panel, k, 3, at(z, y, 1 - c))),
        )

    def y_push(h, t, k):
        panel = at(order(k), 1 - y, c)
        return ((None, push(h, t, cols.at[h, panel, t], panel, k, 4, at(z, y, 1 - c))),)

    def mate_push(h, src, slot, lane, target):
        return pltpu.make_async_remote_copy(
            src_ref=src, dst_ref=mate.at[h, slot], send_sem=mate_send.at[h, lane],
            recv_sem=mate_recv.at[h, slot], device_id={"wide": target}, device_id_type=MESH,
        )

    def beside_push(h):
        return ((None, mate_push(h, own.at[h, nb], 0, 0, at(z, y, 1 - c))),)

    def end_push(h):
        slot = jnp.where(z == 0, 1, 2)
        inward = jnp.where(z == 0, z + 1, z - 1)
        return ((inner == 0, mate_push(h, own.at[h, nb], slot, 1, at(inward, y, c))),)

    def relay_push(h, end, lane):
        onward = jnp.where(end == 0, z + 1, z - 1)
        return ((inner == 1, mate_push(h, mate.at[h, 1 + end], 1 + end, lane, at(onward, y, c))),)

    def far_push(h):
        return ((None, mate_push(h, mate.at[h, 1 + far], 3, 4, at(z, y, 1 - c))),)

    def mate_arrive(h, slot):
        mate_push(h, mate.at[h, slot], slot, 0, at(z, y, 1 - c)).wait_recv()

    def start(pushes):
        for when, copy in pushes:
            if when is None:
                copy.start()
            else:
                pl.when(when)(copy.start)

    def drain(pushes):
        for when, copy in pushes:
            if when is None:
                copy.wait_send()
            else:
                pl.when(when)(copy.wait_send)

    def forward_z(k):
        for t in range(per):
            for h in (b, nb):
                arrive(h, t, at(order(k), y, c))
                start(z_pushes(h, t, k))

    def relay_near(h):
        @pl.when(inner == 1)
        def _():
            mate_arrive(h, 2 - far)
            start(relay_push(h, 1 - far, 2))

    def relay_far(h):
        mate_arrive(h, 1 + far)
        start(relay_push(h, far, 3))
        start(far_push(h))

    def swap(h, i, t):
        p = (nb, b)[i] if h is b else (b, nb)[i]
        return pltpu.make_async_remote_copy(
            src_ref=own.at[h, p, t], dst_ref=own.at[h, p, t], send_sem=own_send.at[i, t],
            recv_sem=own_recv.at[i, t], device_id={"blk": nb}, device_id_type=MESH,
        )

    def hand(panel, u):
        return pltpu.make_async_remote_copy(
            src_ref=stage.at[panel, u], dst_ref=landed.at[panel, u],
            send_sem=res_send.at[panel, u], recv_sem=res_recv.at[panel, u],
            device_id={"blk": nb}, device_id_type=MESH,
        )

    def gram(p, side):
        total = None
        for h in range(2):
            for a in range(2):
                left = own[h, p, :, a].reshape(per * tile, -1)
                right = side(h, 1 - a).reshape(-1, own.shape[5])
                part = lax.dot_general(
                    left, right, (((1,), (1,)), ((), ())), preferred_element_type=jnp.float32
                )
                total = part if total is None else total + part
        return total * scale

    def finish(p, panel, u, part, diagonal):
        for t in range(per):
            slot = panel * per + u
            weight = held[t, p, slot]
            half = part(t) + RIDGE * weight
            if diagonal and t == u:
                rows = lax.broadcasted_iota(jnp.int32, (tile, tile), 0)
                columns = lax.broadcasted_iota(jnp.int32, (tile, tile), 1)
                on_diag = rows == columns + b * (2 * tile)
                inverse = jnp.where(on_diag, 1.0 / jnp.where(on_diag, weight, 1.0), 0.0)
                stepped = weight - STEP * (half - inverse)
            else:
                stepped = weight - STEP * half
            bound = STEP * LASSO
            updated = stepped - jnp.clip(stepped, -bound, bound)
            if diagonal and t == u:
                updated = jnp.where(on_diag, stepped, updated)
            flag = flags[2 * t + p, slot].astype(jnp.float32)
            held[t, p, slot] = updated * flag

    def cut(total, u=0):
        return lambda t: total[t * tile:(t + 1) * tile, u * tile:(u + 1) * tile]

    def finish_all(p, panel, total, diagonal):
        for u in range(per):
            finish(p, panel, u, cut(total, u), diagonal)

    for load in loads:
        load.wait()
    for i in range(2):
        for t in range(per):
            swap(b, i, t).start()
    for t in range(per):
        start(own_pushes(b, t))
    load_weights.start()
    for t in range(per):
        swap(nb, 0, t).wait_recv()
        start(own_pushes(nb, t))
    start(end_push(b))
    start(beside_push(b))
    for h in (b, nb):
        for t in range(per):
            arrive(h, t, at(order(1), y, c))
            start(z_pushes(h, t, 1))

            @pl.when(inner == 1)
            def _():
                arrive(h, t, at(order(2), y, c))
                start(z_pushes(h, t, 2)[:1])
    for t in range(per):
        swap(nb, 1, t).wait_recv()
    start(end_push(nb))
    load_weights.wait()

    def place(n):
        s = n + 2 + jnp.where(n < 4 * depth - 6, 0, 2)
        k, i = s // 4, s % 4
        yy = jnp.where(i < 2, y, 1 - y)
        cc = jnp.where(i % 2 == 0, c, 1 - c)
        return k, i, at(order(k), yy, cc)

    steps = 4 * depth - 4
    middle = steps - 4

    def receive(n, carry):
        panel = place(n)[2]
        for u in range(per):
            hand(panel, u).wait_recv()
            finish(1, panel, u, lambda t: landed[panel, u, t], False)
        return carry

    def keep(panel):
        finish_all(0, panel, gram(0, lambda h, a: cols[h, panel, :, a]), False)

    def nearby():
        for p in range(2):
            parity = b if p == 0 else nb
            finish_all(p, w, gram(p, lambda h, a: own[h, parity, :, a]), True)
        panel = at(z, y, 1 - c)
        for h in (b, nb):
            for t in range(per):
                arrive(h, t, panel)
            mate_arrive(h, 0)
        keep(panel)
        finish_all(1, panel, gram(1, lambda h, a: mate[h, 0, :, a]), False)

    def compute(n, carry):
        k, i, panel = place(n)
        ahead = k + 1 + inner

        @pl.when(jnp.logical_and(i == 2, k == 1))
        def _():
            nearby()

        @pl.when(jnp.logical_and(n == 0, inner == 1))
        def _():
            for t in range(per):
                for h in (b, nb):
                    start(z_pushes(h, t, 2)[1:])

        @pl.when(jnp.logical_and(i == 2, jnp.logical_and(k > 0, ahead < depth)))
        def _():
            forward_z(ahead)

        @pl.when(jnp.logical_and(i == 2, k == 1))
        def _():
            relay_near(b)

        @pl.when(jnp.logical_and(i == 2, k == last - inner))
        def _():
            relay_far(b)

        @pl.when(jnp.logical_and(i == 2, k == last))
        def _():
            lax.fori_loop(0, middle, receive, 0)

        for u in range(per):
            @pl.when(i != 0)
            def _():
                for h in (b, nb):
                    arrive(h, u, panel)

            @pl.when(i == 2)
            def _():
                for h in (b, nb):
                    start(y_push(h, u, k))

            total = cut(gram(1, lambda h, a: cols[h, panel, u, a]))
            for t in range(per):
                stage[panel, u, t] = total(t)
            hand(panel, u).start()

        @pl.when(n == 0)
        def _():
            start(beside_push(nb))

        @pl.when(k < last)
        def _():
            keep(panel)

        @pl.when(jnp.logical_and(i == 3, k == 1))
        def _():
            relay_near(nb)

        @pl.when(jnp.logical_and(i == 3, jnp.logical_and(k == 2, inner == 1)))
        def _():
            relay_far(nb)

        return carry

    lax.fori_loop(0, steps, compute, 0)

    def keep_late(n, carry):
        keep(place(n)[2])
        return carry

    lax.fori_loop(steps - 2, steps, keep_late, 0)

    @pl.when(inner == 0)
    def _():
        relay_far(nb)

    def distant(n, carry):
        cc = jnp.where(n == 0, c, 1 - c)
        slot = jnp.where(n == 0, 1 + far, 3)
        panel = at(far_z, y, cc)

        @pl.when(n == 1)
        def _():
            for h in (b, nb):
                for t in range(per):
                    arrive(h, t, panel)
                mate_arrive(h, 3)

        keep(panel)
        finish_all(1, panel, gram(1, lambda h, a: mate[h, slot, :, a]), False)
        return carry

    lax.fori_loop(0, 2, distant, 0)
    lax.fori_loop(middle, steps, receive, 0)

    for i in range(2):
        for t in range(per):
            swap(b, i, t).wait_send()
    for h in (b, nb):
        for t in range(per):
            drain(own_pushes(h, t))
        drain(beside_push(h))
        drain(end_push(h))
        drain(relay_push(h, 1 - far, 2))
        drain(relay_push(h, far, 3))
        drain(far_push(h))

    def drain_group(k, carry):
        for h in (b, nb):
            for t in range(per):
                drain(y_push(h, t, k))

                @pl.when(k > 0)
                def _():
                    drain(z_pushes(h, t, k))
        return carry

    lax.fori_loop(0, depth, drain_group, 0)

    def drain_panel(n, carry):
        for u in range(per):
            hand(place(n)[2], u).wait_send()
        return carry

    lax.fori_loop(0, steps, drain_panel, 0)


def ring(resid, samples, precision, active):
    panels = lax.axis_size("wide")
    row_tiles, _, per_class, tile, _ = precision.shape
    per = row_tiles // 2
    half = resid.shape[1]
    depth = panels // 4
    scale = 0.5 / (2 * half)
    any_spec = pl.BlockSpec(memory_space=pl.ANY)
    bf16, f32 = resid.dtype, jnp.float32
    dma = pltpu.SemaphoreType.DMA
    updated = pl.pallas_call(
        functools.partial(kernel, depth, scale),
        out_shape=pltpu.VMEM((per, 2, per_class, tile, tile), f32),
        in_specs=[any_spec, any_spec, any_spec, pl.BlockSpec(memory_space=pltpu.SMEM)],
        out_specs=pl.BlockSpec(memory_space=pltpu.VMEM),
        scratch_shapes=[
            pltpu.VMEM((2, 2, per, 2, tile, half), bf16),
            pltpu.VMEM((2, panels, per, 2, tile, half), bf16),
            pltpu.VMEM((2, 4, per, 2, tile, half), bf16),
            pltpu.VMEM((panels, per, per, tile, tile), f32),
            pltpu.VMEM((panels, per, per, tile, tile), f32),
            dma((2, panels, per)),
            dma((2, per)),
            dma((panels, per)),
            dma((2, 4)),
            dma((2, per, depth, 5)),
            dma((2, per)),
            dma((panels, per)),
            dma((2, 5)),
            dma((5,)),
        ],
        compiler_params=pltpu.CompilerParams(
            collective_id=0, has_side_effects=True, vmem_limit_bytes=52 * 1024 * 1024
        ),
    )(
        resid.reshape(per, 2, tile, half),
        samples.reshape(per, 2, tile, half),
        precision.reshape(per, 2, per_class, tile, tile),
        active[:, 0],
    )
    return updated.reshape(precision.shape)


def body(resid, samples, precision, active):
    panels = lax.axis_size("wide")
    row_tiles, _, per_class, tile, _ = precision.shape
    words = 8 * per_class * row_tiles * tile * tile + 4 * panels * row_tiles * tile * resid.shape[1]
    if lax.axis_size("blk") == 2 and panels // 4 == 4 and row_tiles % 2 == 0 and words < 52 * 1024 * 1024:
        return ring(resid, samples, precision, active)
    return local(resid, samples, precision, active)


def solution(mesh):
    in_specs = (
        P("wide", "blk"),
        P("wide", "blk"),
        P("wide", "blk", None, None, None),
        P("wide", "blk", None),
    )
    out_specs = P("wide", "blk", None, None, None)
    return jax.shard_map(body, mesh=mesh, in_specs=in_specs, out_specs=out_specs, check_vma=False)
```
